128 devices in a mesh: rows: 32 (over x, z, core), rel: 4 (over y).
Axes of the slice: x: 4, y: 4, z: 4, core: 2. Of those that a mesh axis runs over, the one named last changes fastest.
Arguments:
- features: bfloat16 [16384, 256], P('rows'), may hold values from -6 to 6
- bases: bfloat16 [8, 256, 256], replicated, may hold values from -0.125 to 0.125
- root: bfloat16 [256, 256], replicated, may hold values from -0.375 to 0.375
- coeffs: float32 [800, 8], P('rel'), may hold values from -4 to 4
- tiles: bfloat16 [32, 4, 64, 128, 128], P('rows', 'rel'), as said below
- tile_dst: int32 [32, 4, 64], P('rows', 'rel'), may hold values from 0 to 3
- tile_src: int32 [32, 4, 64], P('rows', 'rel'), may hold values from 0 to 63
- tile_rel: int32 [32, 4, 64], P('rows', 'rel'), may hold values from 0 to 199
- tile_live: int32 [32, 4], P('rows', 'rel'), may hold values from 16 to 64, as said below
- send_list: int32 [32, 4, 32, 2], P('rows', 'rel'), may hold values from 0 to 3
- cotangent: bfloat16 [16384, 256], P('rows'), may hold values from -6 to 6
Outputs:
- output: bfloat16 [16384, 256], P('rows')
- feature_grad: float32 [16384, 256], P('rows')
- basis_grad: float32 [8, 256, 256], replicated
- root_grad: float32 [256, 256], replicated
The draws below stay inside these ranges and needn't reach their ends.
Inputs may be any that keep to these rules, and one draw needn't show every extreme that they name: `tile_live`: at least one device uses all 64 tile slots. `tiles`: entries are zero or positive, at most 12 / sqrt(2048).
All inputs are finite; a program needn't handle non-finite values.
Results may differ from the reference program's by a relative error of at most 0.0029.
Values may be sent and summed in bfloat16 or wider, within the bound.
A program may use at most 128 MiB of HBM per device.

```python
import math
import jax
import jax.numpy as jnp
import numpy as np
from jax import lax

F = 256
NB = 8
R = 800
BS = 128
LB = 4
TILES = 64
S = 2
RG = 200
N = 16384
N_ROWS = 32
N_REL = 4


def draw_tiles(key, part):
    first, second = jax.random.split(key, 2)
    shape = (N_ROWS, N_REL, TILES, BS, BS)
    present = (jax.random.randint(first, shape, 0, 4) == 0).astype(jnp.float32)
    values = jax.random.uniform(second, shape, jnp.float32, 0.5, 1.5)
    factor = 2.0 / math.sqrt(TILES * BS / LB)
    return (present * values * factor).astype(jnp.bfloat16)


def draw_tile_live(key, part):
    first, second = jax.random.split(key, 2)
    counts = jax.random.randint(first, (N_ROWS * N_REL,), TILES // 4, TILES + 1)
    chosen = jax.random.randint(second, (), 0, N_ROWS * N_REL)
    counts = jnp.where(jnp.arange(N_ROWS * N_REL) == chosen, TILES, counts)
    return counts.reshape(N_ROWS, N_REL).astype(jnp.int32)


def set_ends(array, own_key, least, largest):
    longest = array.shape.index(max(array.shape))
    spots = []
    for shift in (0, 1):
        where = [jax.random.randint(jax.random.fold_in(own_key, axis), (), 0, length) for axis, length in enumerate(array.shape)]
        where[longest] = (where[longest] + shift) % array.shape[longest]
        spots.append(tuple(where))
    return array.at[spots[0]].set(least).at[spots[1]].set(largest)


def shard_levels(key, dims, cuts, least, top_value):
    gain, own = 1.0, jax.random.fold_in(key, 6)
    for axis_at, shards_of in cuts:
        heights = jnp.exp(jax.random.uniform(jax.random.fold_in(own, axis_at), (shards_of,), jnp.float32, least / len(cuts), top_value / len(cuts)))
        gain = gain * jnp.repeat(heights, dims[axis_at] // shards_of).reshape([-1 if axis == axis_at else 1 for axis in range(len(dims))])
    return gain


def cumulative_ranks(number_of, slope):
    loads = [(1 << 20) // math.isqrt(standing ** slope) + 1 for standing in range(1, number_of + 1)]
    scale = 1 + sum(loads) // (1 << 30)
    return np.cumsum(np.array([max(1, weight // scale) for weight in loads]))


def ranked_ids(rng, extent, amount, skew):
    grid = cumulative_ranks(amount, skew)
    ticket = jax.random.randint(jax.random.fold_in(rng, 1), extent, 0, int(grid[amount - 1]))
    rank = jnp.searchsorted(jnp.asarray(grid, jnp.int32), ticket, side="right")
    return jax.random.permutation(jax.random.fold_in(rng, 2), amount)[rank].astype(jnp.int32)


def centred(key, dims, width, reach, pieces=(), kind=jnp.bfloat16):
    entries = width * jax.random.normal(key, dims, jnp.float32)
    if pieces:
        entries = entries * shard_levels(key, dims, pieces, -0.22, 0.18)
    return jnp.clip(entries, -reach, reach).astype(kind)


def setup_inputs(seed: int = 0) -> dict:
    seeds = jax.random.split(jax.random.key(seed), 12)
    return {
        "features": centred(seeds[0], (N, F), 1.0, 6.0, ((0, 32),)),
        "bases": centred(seeds[1], (NB, F, F), (NB * F) ** -0.5, 0.125),
        "root": centred(seeds[2], (F, F), F ** -0.5, 0.375),
        "coeffs": centred(seeds[3], (R, NB), 1.0, 4.0, ((0, 4),), jnp.float32),
        "tiles": draw_tiles(jax.random.fold_in(seeds[11], 71), 0),
        "tile_dst": set_ends(jax.random.randint(seeds[5], (N_ROWS, N_REL, TILES), 0, LB), jax.random.fold_in(seeds[5], 1), 0, LB - 1).astype(jnp.int32),
        "tile_src": set_ends(jax.random.randint(seeds[6], (N_ROWS, N_REL, TILES), 0, N_ROWS * S), jax.random.fold_in(seeds[6], 1), 0, (N_ROWS * S) - 1).astype(jnp.int32),
        "tile_rel": set_ends(ranked_ids(seeds[7], (N_ROWS, N_REL, TILES), RG, 2), jax.random.fold_in(seeds[7], 3), 0, RG - 1).astype(jnp.int32),
        "tile_live": draw_tile_live(jax.random.fold_in(seeds[11], 71), 0),
        "send_list": set_ends(jax.random.randint(seeds[9], (N_ROWS, N_REL, N_ROWS, S), 0, LB), jax.random.fold_in(seeds[9], 1), 0, LB - 1).astype(jnp.int32),
        "cotangent": centred(seeds[10], (N, F), 1.0, 6.0, ((0, 32),)),
    }


def tile_weights(dst_ids, rel_ids, live_count, coef_group):
    in_use = (jnp.arange(TILES) < live_count).astype(jnp.float32)
    coef_rows = coef_group[rel_ids]
    dst_hot = (dst_ids[:, None] == jnp.arange(LB)[None, :]).astype(jnp.float32) * in_use[:, None]
    return (dst_hot[:, :, None] * coef_rows[:, None, :]).reshape(TILES, LB * NB)


def reference(features, bases, root, coeffs, tiles, tile_dst, tile_src, tile_rel, tile_live, send_list, cotangent):
    highest = lax.Precision.HIGHEST
    blocks = features.reshape(N_ROWS, LB, BS, F)
    basis_f = bases.astype(jnp.float32)
    cot_blocks = cotangent.reshape(N_ROWS, LB, BS, F)
    coef_groups = coeffs.reshape(N_REL, RG, NB)
    peer_ids = jnp.arange(N_ROWS, dtype=jnp.int32)[:, None]

    def weights_of(row_index, group_index):
        return tile_weights(tile_dst[row_index, group_index], tile_rel[row_index, group_index],
                            tile_live[row_index, group_index], coef_groups[group_index])

    def forward_row(row_index):
        running = jnp.zeros((LB * NB, BS * F), jnp.float32)
        for group_index in range(N_REL):
            send_rows = send_list[:, group_index, row_index, :]
            received = blocks[peer_ids, send_rows].reshape(N_ROWS * S, BS, F)
            sources = received[tile_src[row_index, group_index]]
            messages = jnp.einsum("tij,tjf->tif", tiles[row_index, group_index].astype(jnp.float32),
                                  sources.astype(jnp.float32))
            running = running + jnp.dot(weights_of(row_index, group_index).T, messages.reshape(TILES, -1),
                                        precision=highest)
        aggregate = running.reshape(LB, NB, BS, F)
        projected = jnp.einsum("lbnf,bfg->lng", aggregate, basis_f, precision=highest)
        root_term = jnp.dot(blocks[row_index].reshape(LB * BS, F), root, preferred_element_type=jnp.float32)
        out_row = (projected.reshape(LB * BS, F) + root_term).astype(jnp.bfloat16)
        grad_row = jnp.einsum("lbnf,lng->bfg", aggregate, cot_blocks[row_index].astype(jnp.float32),
                              precision=highest)
        return out_row, grad_row

    out_rows, grad_rows = lax.map(forward_row, jnp.arange(N_ROWS, dtype=jnp.int32))
    output = out_rows.reshape(N, F)
    basis_grad = jnp.sum(grad_rows, axis=0)
    root_grad = jnp.dot(features.T, cotangent, preferred_element_type=jnp.float32)

    def back_pair(collected, pair_index):
        row_index = pair_index[0]
        group_index = pair_index[1]
        agg_grad = jnp.einsum("lng,bfg->lbnf", cot_blocks[row_index].astype(jnp.float32), basis_f,
                              precision=highest).reshape(LB * NB, BS * F)
        spread = jnp.dot(weights_of(row_index, group_index), agg_grad, precision=highest)
        spread = spread.astype(jnp.bfloat16).reshape(TILES, BS, F)
        backward_term = jnp.einsum("tij,tif->tjf", tiles[row_index, group_index].astype(jnp.float32),
                                   spread.astype(jnp.float32))
        slot_hot = (tile_src[row_index, group_index][:, None] == jnp.arange(N_ROWS * S)[None, :]).astype(jnp.float32)
        slot_grads = jnp.dot(slot_hot.T, backward_term.reshape(TILES, -1), precision=highest)
        slot_grads = slot_grads.reshape(N_ROWS, S, BS, F)
        send_rows = send_list[:, group_index, row_index, :]
        collected = collected.at[peer_ids, send_rows].add(slot_grads)
        return collected, None

    row_list = jnp.repeat(jnp.arange(N_ROWS, dtype=jnp.int32), N_REL)
    group_list = jnp.tile(jnp.arange(N_REL, dtype=jnp.int32), N_ROWS)
    pair_list = jnp.stack([row_list, group_list], axis=1)
    gathered_grads, _ = lax.scan(back_pair, jnp.zeros((N_ROWS, LB, BS, F), jnp.float32), pair_list)
    root_back = lax.dot_general(cotangent, root, (((1,), (1,)), ((), ())), preferred_element_type=jnp.float32)
    feature_grad = gathered_grads.reshape(N, F) + root_back
    return (output, feature_grad, basis_grad, root_grad)
```

```python
import math

import jax
import jax.numpy as jnp
from jax import lax
from jax.sharding import PartitionSpec as P


def on_device(
    features,
    bases,
    root,
    coeffs,
    tiles,
    tile_dst,
    tile_src,
    tile_rel,
    tile_live,
    send_list,
    cotangent,
):
    highest = lax.Precision.HIGHEST
    contract_first = (((0,), (0,)), ((), ()))
    feat_width = features.shape[1]
    size_block = tiles.shape[-1]
    blocks = features.reshape(-1, size_block, feat_width)
    local_blocks = blocks.shape[0]
    num_bases = bases.shape[0]
    slots_peer = send_list.shape[-1]
    row_devices = lax.axis_size("rows")
    total_slots = row_devices * slots_peer
    count_tiles = tiles.shape[2]
    adjacency = tiles[0, 0]
    dst_ids = tile_dst[0, 0]
    src_ids = tile_src[0, 0]
    rel_ids = tile_rel[0, 0]
    live_count = tile_live[0, 0]
    send_rows = send_list[0, 0]
    outgoing = blocks[send_rows]
    incoming = lax.all_to_all(outgoing, "rows", split_axis=0, concat_axis=0, tiled=True)
    received = incoming.reshape(total_slots, size_block, feat_width)
    step_tiles = math.gcd(count_tiles, 64)
    steps_live = (live_count + step_tiles - 1) // step_tiles

    def tile_weights(first_tile):
        position = first_tile + jnp.arange(step_tiles)
        in_use = (position < live_count).astype(jnp.float32)
        rel_hot = (rel_ids[:, None] == jnp.arange(coeffs.shape[0])[None, :]).astype(jnp.float32)
        coef_rows = jnp.dot(rel_hot, coeffs, precision=highest)
        dst_hot = (dst_ids[:, None] == jnp.arange(local_blocks)[None, :]).astype(
            jnp.float32
        ) * in_use[:, None]
        return (dst_hot[:, :, None] * coef_rows[:, None, :]).reshape(
            step_tiles, local_blocks * num_bases
        )

    def forward_step(block_index, running):
        first_tile = block_index * step_tiles
        sources = received[src_ids]
        messages = jnp.einsum(
            "tij,tjf->tif", adjacency, sources, preferred_element_type=jnp.float32
        )
        weights = tile_weights(first_tile)
        return running + lax.dot_general(
            weights, messages.reshape(step_tiles, -1), contract_first, precision=highest
        )

    zero_total = jnp.zeros((local_blocks * num_bases, size_block * feat_width), jnp.float32)
    partial_value = lax.fori_loop(0, steps_live, forward_step, zero_total)
    partial_value = partial_value.reshape(local_blocks, num_bases, size_block, feat_width)
    basis_f32 = bases.astype(jnp.float32)
    cot_blocks = cotangent.reshape(local_blocks, size_block, feat_width)
    cot_f32 = cot_blocks.astype(jnp.float32)
    root_term = jnp.dot(features, root, preferred_element_type=jnp.float32)
    rel_devices = lax.axis_size("rel")
    part_rows = features.shape[0] // rel_devices
    first_row = lax.axis_index("rel") * part_rows
    feat_part = lax.dynamic_slice_in_dim(features, first_row, part_rows)
    cot_part = lax.dynamic_slice_in_dim(cotangent, first_row, part_rows)
    root_local = lax.dot_general(
        feat_part, cot_part, contract_first, preferred_element_type=jnp.float32
    )
    projected_part = jnp.einsum("lbnf,bfg->lng", partial_value, basis_f32, precision=highest)
    basis_local = jnp.einsum("lbnf,lng->bfg", partial_value, cot_f32, precision=highest)
    projected = lax.psum(projected_part, "rel")
    basis_grad, root_grad = lax.psum((basis_local, root_local), ("rows", "rel"))
    output = (projected.reshape(-1, feat_width) + root_term).astype(jnp.bfloat16)
    agg_grad = jnp.einsum("lng,bfg->lbnf", cot_blocks, bases, preferred_element_type=jnp.float32)
    agg_grad = agg_grad.reshape(local_blocks * num_bases, size_block * feat_width)

    def backward_step(block_index, running):
        first_tile = block_index * step_tiles
        weights = tile_weights(first_tile)
        spread = jnp.dot(weights, agg_grad, precision=highest).astype(jnp.bfloat16)
        spread = spread.reshape(step_tiles, size_block, feat_width)
        backward_term = jnp.einsum(
            "tij,tif->tjf", adjacency, spread, preferred_element_type=jnp.float32
        )
        slot_hot = (src_ids[:, None] == jnp.arange(total_slots)[None, :]).astype(jnp.float32)
        return running + lax.dot_general(
            slot_hot, backward_term.reshape(step_tiles, -1), contract_first, precision=highest
        )

    slot_zero = jnp.zeros((total_slots, size_block * feat_width), jnp.float32)
    slot_grads = lax.fori_loop(0, steps_live, backward_step, slot_zero)
    returned = lax.all_to_all(
        slot_grads.reshape(row_devices, slots_peer, size_block * feat_width),
        "rows",
        split_axis=0,
        concat_axis=0,
        tiled=True,
    )
    block_hot = (send_rows.reshape(-1)[None, :] == jnp.arange(local_blocks)[:, None]).astype(
        jnp.float32
    )
    own_grads = jnp.dot(block_hot, returned.reshape(total_slots, -1), precision=highest)
    own_grads, projected = lax.optimization_barrier((own_grads, projected))
    summed = lax.psum(own_grads, "rel")
    root_back = lax.dot_general(
        cotangent, root, (((1,), (1,)), ((), ())), preferred_element_type=jnp.float32
    )
    feature_grad = summed.reshape(-1, feat_width) + root_back
    return (output, feature_grad, basis_grad, root_grad)


def solution(mesh):
    return jax.shard_map(
        on_device,
        mesh=mesh,
        in_specs=(
            P("rows", None),
            P(),
            P(),
            P("rel", None),
            P("rows", "rel", None, None, None),
            P("rows", "rel", None),
            P("rows", "rel", None),
            P("rows", "rel", None),
            P("rows", "rel"),
            P("rows", "rel", None, None),
            P("rows", None),
        ),
        out_specs=(P("rows", None), P("rows", None), P(), P()),
        check_vma=False,
    )
```

```python
import math

import jax
import jax.numpy as jnp
from jax import lax
from jax.sharding import PartitionSpec as P


def a2a_psum(value, axes):
    count = 1
    for name in axes:
        count *= lax.axis_size(name)
    flat = value.reshape(count, -1)
    pieces = lax.all_to_all(flat, axes, 0, 0, tiled=True)
    reduced = jnp.sum(pieces, axis=0, keepdims=True)
    spread_out = jnp.broadcast_to(reduced, flat.shape)
    gathered = lax.all_to_all(spread_out, axes, 0, 0, tiled=True)
    return gathered.reshape(value.shape)


def on_device(
    features,
    bases,
    root,
    coeffs,
    tiles,
    tile_dst,
    tile_src,
    tile_rel,
    tile_live,
    send_list,
    cotangent,
):
    highest = lax.Precision.HIGHEST
    contract_first = (((0,), (0,)), ((), ()))
    feat_width = features.shape[1]
    size_block = tiles.shape[-1]
    blocks = features.reshape(-1, size_block, feat_width)
    local_blocks = blocks.shape[0]
    num_bases = bases.shape[0]
    slots_peer = send_list.shape[-1]
    row_devices = lax.axis_size("rows")
    total_slots = row_devices * slots_peer
    count_tiles = tiles.shape[2]
    adjacency = tiles[0, 0]
    dst_ids = tile_dst[0, 0]
    src_ids = tile_src[0, 0]
    rel_ids = tile_rel[0, 0]
    live_count = tile_live[0, 0]
    send_rows = send_list[0, 0]
    outgoing = blocks[send_rows]
    incoming = lax.all_to_all(outgoing, "rows", split_axis=0, concat_axis=0, tiled=True)
    received = incoming.reshape(total_slots, size_block, feat_width)
    step_tiles = math.gcd(count_tiles, 64)
    steps_live = (live_count + step_tiles - 1) // step_tiles

    def tile_weights(first_tile):
        position = first_tile + jnp.arange(step_tiles)
        in_use = (position < live_count).astype(jnp.float32)
        rel_hot = (rel_ids[:, None] == jnp.arange(coeffs.shape[0])[None, :]).astype(jnp.float32)
        coef_rows = jnp.dot(rel_hot, coeffs, precision=highest)
        dst_hot = (dst_ids[:, None] == jnp.arange(local_blocks)[None, :]).astype(
            jnp.float32
        ) * in_use[:, None]
        return (dst_hot[:, :, None] * coef_rows[:, None, :]).reshape(
            step_tiles, local_blocks * num_bases
        )

    def forward_step(block_index, running):
        first_tile = block_index * step_tiles
        sources = received[src_ids]
        messages = jnp.einsum(
            "tij,tjf->tif", adjacency, sources, preferred_element_type=jnp.float32
        )
        weights = tile_weights(first_tile)
        return running + lax.dot_general(
            weights, messages.reshape(step_tiles, -1), contract_first, precision=highest
        )

    zero_total = jnp.zeros((local_blocks * num_bases, size_block * feat_width), jnp.float32)
    partial_value = lax.fori_loop(0, steps_live, forward_step, zero_total)
    partial_value = partial_value.reshape(local_blocks, num_bases, size_block, feat_width)
    basis_f32 = bases.astype(jnp.float32)
    cot_blocks = cotangent.reshape(local_blocks, size_block, feat_width)
    cot_f32 = cot_blocks.astype(jnp.float32)
    root_term = jnp.dot(features, root, preferred_element_type=jnp.float32)
    rel_devices = lax.axis_size("rel")
    part_rows = features.shape[0] // rel_devices
    first_row = lax.axis_index("rel") * part_rows
    feat_part = lax.dynamic_slice_in_dim(features, first_row, part_rows)
    cot_part = lax.dynamic_slice_in_dim(cotangent, first_row, part_rows)
    root_local = lax.dot_general(
        feat_part, cot_part, contract_first, preferred_element_type=jnp.float32
    )
    projected_part = jnp.einsum("lbnf,bfg->lng", partial_value, basis_f32, precision=highest)
    basis_local = jnp.einsum("lbnf,lng->bfg", partial_value, cot_f32, precision=highest)
    projected = a2a_psum(projected_part, ("rel",))
    grads_flat = jnp.concatenate([basis_local.reshape(-1), root_local.reshape(-1)])
    grads_flat = a2a_psum(grads_flat, ("rows", "rel"))
    basis_grad = grads_flat[: basis_local.size].reshape(basis_local.shape)
    root_grad = grads_flat[basis_local.size :].reshape(root_local.shape)
    output = (projected.reshape(-1, feat_width) + root_term).astype(jnp.bfloat16)
    agg_grad = jnp.einsum("lng,bfg->lbnf", cot_blocks, bases, preferred_element_type=jnp.float32)
    agg_grad = agg_grad.reshape(local_blocks * num_bases, size_block * feat_width)

    def backward_step(block_index, running):
        first_tile = block_index * step_tiles
        weights = tile_weights(first_tile)
        spread = jnp.dot(weights, agg_grad, precision=highest).astype(jnp.bfloat16)
        spread = spread.reshape(step_tiles, size_block, feat_width)
        backward_term = jnp.einsum(
            "tij,tif->tjf", adjacency, spread, preferred_element_type=jnp.float32
        )
        slot_hot = (src_ids[:, None] == jnp.arange(total_slots)[None, :]).astype(jnp.float32)
        return running + lax.dot_general(
            slot_hot, backward_term.reshape(step_tiles, -1), contract_first, precision=highest
        )

    slot_zero = jnp.zeros((total_slots, size_block * feat_width), jnp.float32)
    slot_grads = lax.fori_loop(0, steps_live, backward_step, slot_zero)
    returned = lax.all_to_all(
        slot_grads.reshape(row_devices, slots_peer, size_block * feat_width),
        "rows",
        split_axis=0,
        concat_axis=0,
        tiled=True,
    )
    block_hot = (send_rows.reshape(-1)[None, :] == jnp.arange(local_blocks)[:, None]).astype(
        jnp.float32
    )
    own_grads = jnp.dot(block_hot, returned.reshape(total_slots, -1), precision=highest)
    own_grads, projected = lax.optimization_barrier((own_grads, projected))
    summed = a2a_psum(own_grads, ("rel",))
    root_back = lax.dot_general(
        cotangent, root, (((1,), (1,)), ((), ())), preferred_element_type=jnp.float32
    )
    feature_grad = summed.reshape(-1, feat_width) + root_back
    return (output, feature_grad, basis_grad, root_grad)


def solution(mesh):
    return jax.shard_map(
        on_device,
        mesh=mesh,
        in_specs=(
            P("rows", None),
            P(),
            P(),
            P("rel", None),
            P("rows", "rel", None, None, None),
            P("rows", "rel", None),
            P("rows", "rel", None),
            P("rows", "rel", None),
            P("rows", "rel"),
            P("rows", "rel", None, None),
            P("rows", None),
        ),
        out_specs=(P("rows", None), P("rows", None), P(), P()),
        check_vma=False,
    )
```

```python
import math

import jax
import jax.numpy as jnp
from jax import lax
from jax.sharding import PartitionSpec as P

SLOT_GRAD_LINK_DTYPE = jnp.float32


def a2a_psum(value, axes):
    count = 1
    for name in axes:
        count *= lax.axis_size(name)
    flat = value.reshape(count, -1)
    pieces = lax.all_to_all(flat, axes, 0, 0, tiled=True)
    reduced = jnp.sum(pieces, axis=0, keepdims=True)
    spread_out = jnp.broadcast_to(reduced, flat.shape)
    gathered = lax.all_to_all(spread_out, axes, 0, 0, tiled=True)
    return gathered.reshape(value.shape)


def on_device(
    features,
    bases,
    root,
    coeffs,
    tiles,
    tile_dst,
    tile_src,
    tile_rel,
    tile_live,
    send_list,
    cotangent,
):
    highest = lax.Precision.HIGHEST
    contract_first = (((0,), (0,)), ((), ()))
    feat_width = features.shape[1]
    size_block = tiles.shape[-1]
    blocks = features.reshape(-1, size_block, feat_width)
    local_blocks = blocks.shape[0]
    num_bases = bases.shape[0]
    slots_peer = send_list.shape[-1]
    row_devices = lax.axis_size("rows")
    total_slots = row_devices * slots_peer
    count_tiles = tiles.shape[2]
    adjacency = tiles[0, 0]
    dst_ids = tile_dst[0, 0]
    src_ids = tile_src[0, 0]
    rel_ids = tile_rel[0, 0]
    live_count = tile_live[0, 0]
    send_rows = send_list[0, 0]
    step_tiles = math.gcd(count_tiles, 64)
    steps_live = (live_count + step_tiles - 1) // step_tiles

    def tile_weights(first_tile):
        position = first_tile + jnp.arange(step_tiles)
        in_use = (position < live_count).astype(jnp.float32)
        rel_hot = (rel_ids[:, None] == jnp.arange(coeffs.shape[0])[None, :]).astype(jnp.float32)
        coef_rows = jnp.dot(rel_hot, coeffs, precision=highest)
        dst_hot = (dst_ids[:, None] == jnp.arange(local_blocks)[None, :]).astype(
            jnp.float32
        ) * in_use[:, None]
        return (dst_hot[:, :, None] * coef_rows[:, None, :]).reshape(
            step_tiles, local_blocks * num_bases
        )

    outgoing = blocks[send_rows]
    incoming = lax.all_to_all(outgoing, "rows", split_axis=0, concat_axis=0, tiled=True)

    cot_blocks = cotangent.reshape(local_blocks, size_block, feat_width)
    agg_grad = jnp.einsum("lng,bfg->lbnf", cot_blocks, bases, preferred_element_type=jnp.float32)
    agg_grad = agg_grad.reshape(local_blocks * num_bases, size_block * feat_width)

    def backward_step(block_index, running):
        first_tile = block_index * step_tiles
        weights = tile_weights(first_tile)
        spread = jnp.dot(weights, agg_grad, precision=highest).astype(jnp.bfloat16)
        spread = spread.reshape(step_tiles, size_block, feat_width)
        backward_term = jnp.einsum(
            "tij,tif->tjf", adjacency, spread, preferred_element_type=jnp.float32
        )
        slot_hot = (src_ids[:, None] == jnp.arange(total_slots)[None, :]).astype(jnp.float32)
        return running + lax.dot_general(
            slot_hot, backward_term.reshape(step_tiles, -1), contract_first, precision=highest
        )

    slot_zero = jnp.zeros((total_slots, size_block * feat_width), jnp.float32)
    slot_grads = lax.fori_loop(0, steps_live, backward_step, slot_zero)
    incoming, slot_grads = lax.optimization_barrier((incoming, slot_grads))

    returned = lax.all_to_all(
        slot_grads.astype(SLOT_GRAD_LINK_DTYPE).reshape(
            row_devices, slots_peer, size_block * feat_width
        ),
        "rows",
        split_axis=0,
        concat_axis=0,
        tiled=True,
    )

    received = incoming.reshape(total_slots, size_block, feat_width)

    def forward_step(block_index, running):
        first_tile = block_index * step_tiles
        sources = received[src_ids]
        messages = jnp.einsum(
            "tij,tjf->tif", adjacency, sources, preferred_element_type=jnp.float32
        )
        weights = tile_weights(first_tile)
        return running + lax.dot_general(
            weights, messages.reshape(step_tiles, -1), contract_first, precision=highest
        )

    zero_total = jnp.zeros((local_blocks * num_bases, size_block * feat_width), jnp.float32)
    partial_value = lax.fori_loop(0, steps_live, forward_step, zero_total)
    partial_value = partial_value.reshape(local_blocks, num_bases, size_block, feat_width)
    basis_f32 = bases.astype(jnp.float32)
    cot_f32 = cot_blocks.astype(jnp.float32)
    root_term = jnp.dot(features, root, preferred_element_type=jnp.float32)
    rel_devices = lax.axis_size("rel")
    part_rows = features.shape[0] // rel_devices
    first_row = lax.axis_index("rel") * part_rows
    feat_part = lax.dynamic_slice_in_dim(features, first_row, part_rows)
    cot_part = lax.dynamic_slice_in_dim(cotangent, first_row, part_rows)
    root_local = lax.dot_general(
        feat_part, cot_part, contract_first, preferred_element_type=jnp.float32
    )
    projected_part = jnp.einsum("lbnf,bfg->lng", partial_value, basis_f32, precision=highest)
    basis_local = jnp.einsum("lbnf,lng->bfg", partial_value, cot_f32, precision=highest)
    returned, projected_part, basis_local, root_local = lax.optimization_barrier(
        (returned, projected_part, basis_local, root_local)
    )

    projected = a2a_psum(projected_part, ("rel",))
    output = (projected.reshape(-1, feat_width) + root_term).astype(jnp.bfloat16)
    grads_flat = jnp.concatenate([basis_local.reshape(-1), root_local.reshape(-1)])
    grads_flat = a2a_psum(grads_flat, ("rows", "rel"))
    basis_grad = grads_flat[: basis_local.size].reshape(basis_local.shape)
    root_grad = grads_flat[basis_local.size :].reshape(root_local.shape)

    block_hot = (send_rows.reshape(-1)[None, :] == jnp.arange(local_blocks)[:, None]).astype(
        jnp.float32
    )
    own_grads = jnp.dot(
        block_hot, returned.astype(jnp.float32).reshape(total_slots, -1), precision=highest
    )
    summed = a2a_psum(own_grads, ("rel",))
    root_back = lax.dot_general(
        cotangent, root, (((1,), (1,)), ((), ())), preferred_element_type=jnp.float32
    )
    feature_grad = summed.reshape(-1, feat_width) + root_back
    return (output, feature_grad, basis_grad, root_grad)


def solution(mesh):
    return jax.shard_map(
        on_device,
        mesh=mesh,
        in_specs=(
            P("rows", None),
            P(),
            P(),
            P("rel", None),
            P("rows", "rel", None, None, None),
            P("rows", "rel", None),
            P("rows", "rel", None),
            P("rows", "rel", None),
            P("rows", "rel"),
            P("rows", "rel", None, None),
            P("rows", None),
        ),
        out_specs=(P("rows", None), P("rows", None), P(), P()),
        check_vma=False,
    )
```

```python
import math

import jax
import jax.numpy as jnp
from jax import lax
from jax.sharding import PartitionSpec as P

SLOT_GRAD_LINK_DTYPE = jnp.bfloat16


def a2a_psum(value, axes):
    count = 1
    for name in axes:
        count *= lax.axis_size(name)
    flat = value.reshape(count, -1)
    pieces = lax.all_to_all(flat, axes, 0, 0, tiled=True)
    reduced = jnp.sum(pieces, axis=0, keepdims=True)
    spread_out = jnp.broadcast_to(reduced, flat.shape)
    gathered = lax.all_to_all(spread_out, axes, 0, 0, tiled=True)
    return gathered.reshape(value.shape)


def on_device(
    features,
    bases,
    root,
    coeffs,
    tiles,
    tile_dst,
    tile_src,
    tile_rel,
    tile_live,
    send_list,
    cotangent,
):
    highest = lax.Precision.HIGHEST
    contract_first = (((0,), (0,)), ((), ()))
    feat_width = features.shape[1]
    size_block = tiles.shape[-1]
    blocks = features.reshape(-1, size_block, feat_width)
    local_blocks = blocks.shape[0]
    num_bases = bases.shape[0]
    slots_peer = send_list.shape[-1]
    row_devices = lax.axis_size("rows")
    total_slots = row_devices * slots_peer
    count_tiles = tiles.shape[2]
    adjacency = tiles[0, 0]
    dst_ids = tile_dst[0, 0]
    src_ids = tile_src[0, 0]
    rel_ids = tile_rel[0, 0]
    live_count = tile_live[0, 0]
    send_rows = send_list[0, 0]
    step_tiles = math.gcd(count_tiles, 64)
    steps_live = (live_count + step_tiles - 1) // step_tiles

    def tile_weights(first_tile):
        position = first_tile + jnp.arange(step_tiles)
        in_use = (position < live_count).astype(jnp.float32)
        rel_hot = (rel_ids[:, None] == jnp.arange(coeffs.shape[0])[None, :]).astype(jnp.float32)
        coef_rows = jnp.dot(rel_hot, coeffs, precision=highest)
        dst_hot = (dst_ids[:, None] == jnp.arange(local_blocks)[None, :]).astype(
            jnp.float32
        ) * in_use[:, None]
        return (dst_hot[:, :, None] * coef_rows[:, None, :]).reshape(
            step_tiles, local_blocks * num_bases
        )

    outgoing = blocks[send_rows]
    incoming = lax.all_to_all(outgoing, "rows", split_axis=0, concat_axis=0, tiled=True)

    cot_blocks = cotangent.reshape(local_blocks, size_block, feat_width)
    agg_grad = jnp.einsum("lng,bfg->lbnf", cot_blocks, bases, preferred_element_type=jnp.float32)
    agg_grad = agg_grad.reshape(local_blocks * num_bases, size_block * feat_width)

    def backward_step(block_index, running):
        first_tile = block_index * step_tiles
        weights = tile_weights(first_tile)
        spread = jnp.dot(weights, agg_grad, precision=highest).astype(jnp.bfloat16)
        spread = spread.reshape(step_tiles, size_block, feat_width)
        backward_term = jnp.einsum(
            "tij,tif->tjf", adjacency, spread, preferred_element_type=jnp.float32
        )
        slot_hot = (src_ids[:, None] == jnp.arange(total_slots)[None, :]).astype(jnp.float32)
        return running + lax.dot_general(
            slot_hot, backward_term.reshape(step_tiles, -1), contract_first, precision=highest
        )

    slot_zero = jnp.zeros((total_slots, size_block * feat_width), jnp.float32)
    slot_grads = lax.fori_loop(0, steps_live, backward_step, slot_zero)
    incoming, slot_grads = lax.optimization_barrier((incoming, slot_grads))

    returned = lax.all_to_all(
        slot_grads.astype(SLOT_GRAD_LINK_DTYPE).reshape(
            row_devices, slots_peer, size_block * feat_width
        ),
        "rows",
        split_axis=0,
        concat_axis=0,
        tiled=True,
    )

    received = incoming.reshape(total_slots, size_block, feat_width)

    def forward_step(block_index, running):
        first_tile = block_index * step_tiles
        sources = received[src_ids]
        messages = jnp.einsum(
            "tij,tjf->tif", adjacency, sources, preferred_element_type=jnp.float32
        )
        weights = tile_weights(first_tile)
        return running + lax.dot_general(
            weights, messages.reshape(step_tiles, -1), contract_first, precision=highest
        )

    zero_total = jnp.zeros((local_blocks * num_bases, size_block * feat_width), jnp.float32)
    partial_value = lax.fori_loop(0, steps_live, forward_step, zero_total)
    partial_value = partial_value.reshape(local_blocks, num_bases, size_block, feat_width)
    basis_f32 = bases.astype(jnp.float32)
    cot_f32 = cot_blocks.astype(jnp.float32)
    root_term = jnp.dot(features, root, preferred_element_type=jnp.float32)
    rel_devices = lax.axis_size("rel")
    part_rows = features.shape[0] // rel_devices
    first_row = lax.axis_index("rel") * part_rows
    feat_part = lax.dynamic_slice_in_dim(features, first_row, part_rows)
    cot_part = lax.dynamic_slice_in_dim(cotangent, first_row, part_rows)
    root_local = lax.dot_general(
        feat_part, cot_part, contract_first, preferred_element_type=jnp.float32
    )
    projected_part = jnp.einsum("lbnf,bfg->lng", partial_value, basis_f32, precision=highest)
    basis_local = jnp.einsum("lbnf,lng->bfg", partial_value, cot_f32, precision=highest)
    returned, projected_part, basis_local, root_local = lax.optimization_barrier(
        (returned, projected_part, basis_local, root_local)
    )

    projected = a2a_psum(projected_part, ("rel",))
    output = (projected.reshape(-1, feat_width) + root_term).astype(jnp.bfloat16)
    grads_flat = jnp.concatenate([basis_local.reshape(-1), root_local.reshape(-1)])
    grads_flat = a2a_psum(grads_flat, ("rows", "rel"))
    basis_grad = grads_flat[: basis_local.size].reshape(basis_local.shape)
    root_grad = grads_flat[basis_local.size :].reshape(root_local.shape)

    block_hot = (send_rows.reshape(-1)[None, :] == jnp.arange(local_blocks)[:, None]).astype(
        jnp.float32
    )
    own_grads = jnp.dot(
        block_hot, returned.astype(jnp.float32).reshape(total_slots, -1), precision=highest
    )
    summed = a2a_psum(own_grads, ("rel",))
    root_back = lax.dot_general(
        cotangent, root, (((1,), (1,)), ((), ())), preferred_element_type=jnp.float32
    )
    feature_grad = summed.reshape(-1, feat_width) + root_back
    return (output, feature_grad, basis_grad, root_grad)


def solution(mesh):
    return jax.shard_map(
        on_device,
        mesh=mesh,
        in_specs=(
            P("rows", None),
            P(),
            P(),
            P("rel", None),
            P("rows", "rel", None, None, None),
            P("rows", "rel", None),
            P("rows", "rel", None),
            P("rows", "rel", None),
            P("rows", "rel"),
            P("rows", "rel", None, None),
            P("rows", None),
        ),
        out_specs=(P("rows", None), P("rows", None), P(), P()),
        check_vma=False,
    )
```

```python
import math

import jax
import jax.numpy as jnp
from jax import lax
from jax.sharding import PartitionSpec as P

SLOT_GRAD_LINK_DTYPE = jnp.bfloat16


def a2a_psum(value, axes):
    count = 1
    for name in axes:
        count *= lax.axis_size(name)
    chunked = value.reshape((count, value.shape[0] // count) + value.shape[1:])
    pieces = lax.all_to_all(chunked, axes, 0, 0, tiled=True)
    reduced = jnp.sum(pieces, axis=0, keepdims=True)
    gathered = lax.all_to_all(jnp.broadcast_to(reduced, chunked.shape), axes, 0, 0, tiled=True)
    return gathered.reshape(value.shape)


def on_device(
    features,
    bases,
    root,
    coeffs,
    tiles,
    tile_dst,
    tile_src,
    tile_rel,
    tile_live,
    send_list,
    cotangent,
):
    highest = lax.Precision.HIGHEST
    contract_first = (((0,), (0,)), ((), ()))
    feat_width = features.shape[1]
    size_block = tiles.shape[-1]
    blocks = features.reshape(-1, size_block, feat_width)
    local_blocks = blocks.shape[0]
    num_bases = bases.shape[0]
    slots_peer = send_list.shape[-1]
    row_devices = lax.axis_size("rows")
    total_slots = row_devices * slots_peer
    count_tiles = tiles.shape[2]
    adjacency = tiles[0, 0]
    dst_ids = tile_dst[0, 0]
    src_ids = tile_src[0, 0]
    rel_ids = tile_rel[0, 0]
    live_count = tile_live[0, 0]
    send_rows = send_list[0, 0]
    step_tiles = math.gcd(count_tiles, 64)
    steps_live = (live_count + step_tiles - 1) // step_tiles

    def tile_weights(first_tile):
        position = first_tile + jnp.arange(step_tiles)
        in_use = (position < live_count).astype(jnp.float32)
        rel_hot = (rel_ids[:, None] == jnp.arange(coeffs.shape[0])[None, :]).astype(jnp.float32)
        coef_rows = jnp.dot(rel_hot, coeffs, precision=highest)
        dst_hot = (dst_ids[:, None] == jnp.arange(local_blocks)[None, :]).astype(
            jnp.float32
        ) * in_use[:, None]
        return (dst_hot[:, :, None] * coef_rows[:, None, :]).reshape(
            step_tiles, local_blocks * num_bases
        )

    outgoing = blocks[send_rows]
    incoming = lax.all_to_all(outgoing, "rows", split_axis=0, concat_axis=0, tiled=True)

    cot_blocks = cotangent.reshape(local_blocks, size_block, feat_width)
    agg_grad = jnp.einsum("lng,bfg->lbnf", cot_blocks, bases, preferred_element_type=jnp.float32)
    agg_grad = agg_grad.reshape(local_blocks * num_bases, size_block, feat_width)

    def backward_step(block_index, running):
        first_tile = block_index * step_tiles
        weights = tile_weights(first_tile)
        spread = lax.dot_general(
            weights, agg_grad, (((1,), (0,)), ((), ())), precision=highest
        ).astype(jnp.bfloat16)
        backward_term = jnp.einsum(
            "tij,tif->tjf", adjacency, spread, preferred_element_type=jnp.float32
        )
        slot_hot = (src_ids[:, None] == jnp.arange(total_slots)[None, :]).astype(jnp.float32)
        return running + lax.dot_general(
            slot_hot, backward_term, contract_first, precision=highest
        )

    slot_zero = jnp.zeros((total_slots, size_block, feat_width), jnp.float32)
    slot_grads = lax.fori_loop(0, steps_live, backward_step, slot_zero)
    incoming, slot_grads = lax.optimization_barrier((incoming, slot_grads))

    returned = lax.all_to_all(
        slot_grads.astype(SLOT_GRAD_LINK_DTYPE).reshape(
            row_devices, slots_peer * size_block, feat_width
        ),
        "rows",
        split_axis=0,
        concat_axis=0,
        tiled=True,
    )

    received = incoming.reshape(total_slots, size_block, feat_width)

    def forward_step(block_index, running):
        first_tile = block_index * step_tiles
        sources = received[src_ids]
        messages = jnp.einsum(
            "tij,tjf->tif", adjacency, sources, preferred_element_type=jnp.float32
        )
        weights = tile_weights(first_tile)
        return running + lax.dot_general(
            weights, messages, contract_first, precision=highest
        )

    zero_total = jnp.zeros((local_blocks * num_bases, size_block, feat_width), jnp.float32)
    partial_value = lax.fori_loop(0, steps_live, forward_step, zero_total)
    partial_value = partial_value.reshape(local_blocks, num_bases, size_block, feat_width)
    basis_f32 = bases.astype(jnp.float32)
    cot_f32 = cot_blocks.astype(jnp.float32)
    root_term = jnp.dot(features, root, preferred_element_type=jnp.float32)
    root_local = lax.dot_general(
        features, cotangent, contract_first, preferred_element_type=jnp.float32
    )
    projected_part = jnp.einsum("lbnf,bfg->lng", partial_value, basis_f32, precision=highest)
    basis_local = jnp.einsum("lbnf,lng->bfg", partial_value, cot_f32, precision=highest)
    projected = lax.psum(projected_part, "rel")
    root_grad = lax.psum(root_local, "rows")
    returned, basis_local, projected, root_grad = lax.optimization_barrier(
        (returned, basis_local, projected, root_grad)
    )

    output = (projected.reshape(-1, feat_width) + root_term).astype(jnp.bfloat16)
    basis_grad = a2a_psum(
        basis_local.reshape(-1, basis_local.shape[-1]), ("rows", "rel")
    ).reshape(basis_local.shape)

    block_hot = (send_rows.reshape(-1)[None, :] == jnp.arange(local_blocks)[:, None]).astype(
        jnp.float32
    )
    own_grads = lax.dot_general(
        block_hot,
        returned.astype(jnp.float32).reshape(total_slots, size_block, feat_width),
        (((1,), (0,)), ((), ())),
        precision=highest,
    )
    summed = a2a_psum(own_grads.reshape(-1, feat_width), ("rel",))
    root_back = lax.dot_general(
        cotangent, root, (((1,), (1,)), ((), ())), preferred_element_type=jnp.float32
    )
    feature_grad = summed.reshape(-1, feat_width) + root_back
    return (output, feature_grad, basis_grad, root_grad)


def solution(mesh):
    return jax.shard_map(
        on_device,
        mesh=mesh,
        in_specs=(
            P("rows", None),
            P(),
            P(),
            P("rel", None),
            P("rows", "rel", None, None, None),
            P("rows", "rel", None),
            P("rows", "rel", None),
            P("rows", "rel", None),
            P("rows", "rel"),
            P("rows", "rel", None, None),
            P("rows", None),
        ),
        out_specs=(P("rows", None), P("rows", None), P(), P()),
        check_vma=False,
    )
```

```python
import math

import jax
import jax.numpy as jnp
from jax import lax
from jax.sharding import PartitionSpec as P

SLOT_GRAD_LINK_DTYPE = jnp.bfloat16


def a2a_psum(value, axes):
    count = 1
    for name in axes:
        count *= lax.axis_size(name)
    chunked = value.reshape((count, value.shape[0] // count) + value.shape[1:])
    pieces = lax.all_to_all(chunked, axes, 0, 0, tiled=True)
    reduced = jnp.sum(pieces, axis=0, keepdims=True)
    gathered = lax.all_to_all(jnp.broadcast_to(reduced, chunked.shape), axes, 0, 0, tiled=True)
    return gathered.reshape(value.shape)


def on_device(
    features,
    bases,
    root,
    coeffs,
    tiles,
    tile_dst,
    tile_src,
    tile_rel,
    tile_live,
    send_list,
    cotangent,
):
    highest = lax.Precision.HIGHEST
    contract_first = (((0,), (0,)), ((), ()))
    feat_width = features.shape[1]
    size_block = tiles.shape[-1]
    blocks = features.reshape(-1, size_block, feat_width)
    local_blocks = blocks.shape[0]
    num_bases = bases.shape[0]
    slots_peer = send_list.shape[-1]
    row_devices = lax.axis_size("rows")
    total_slots = row_devices * slots_peer
    count_tiles = tiles.shape[2]
    adjacency = tiles[0, 0]
    dst_ids = tile_dst[0, 0]
    src_ids = tile_src[0, 0]
    rel_ids = tile_rel[0, 0]
    live_count = tile_live[0, 0]
    send_rows = send_list[0, 0]
    step_tiles = math.gcd(count_tiles, 64)
    steps_live = (live_count + step_tiles - 1) // step_tiles

    def tile_weights(first_tile):
        position = first_tile + jnp.arange(step_tiles)
        in_use = (position < live_count).astype(jnp.float32)
        rel_hot = (rel_ids[:, None] == jnp.arange(coeffs.shape[0])[None, :]).astype(jnp.float32)
        coef_rows = jnp.dot(rel_hot, coeffs, precision=highest)
        dst_hot = (dst_ids[:, None] == jnp.arange(local_blocks)[None, :]).astype(
            jnp.float32
        ) * in_use[:, None]
        return (dst_hot[:, :, None] * coef_rows[:, None, :]).reshape(
            step_tiles, local_blocks * num_bases
        )

    outgoing = blocks[send_rows]
    incoming = lax.all_to_all(outgoing, "rows", split_axis=0, concat_axis=0, tiled=True)

    cot_blocks = cotangent.reshape(local_blocks, size_block, feat_width)
    agg_grad = jnp.einsum("lng,bfg->lbnf", cot_blocks, bases, preferred_element_type=jnp.float32)
    agg_grad = agg_grad.reshape(local_blocks * num_bases, size_block, feat_width)

    def backward_step(block_index, running):
        first_tile = block_index * step_tiles
        weights = tile_weights(first_tile)
        spread = lax.dot_general(
            weights, agg_grad, (((1,), (0,)), ((), ())), precision=highest
        ).astype(jnp.bfloat16)
        backward_term = jnp.einsum(
            "tij,tif->tjf", adjacency, spread, preferred_element_type=jnp.float32
        )
        slot_hot = (src_ids[:, None] == jnp.arange(total_slots)[None, :]).astype(jnp.float32)
        return running + lax.dot_general(
            slot_hot, backward_term, contract_first, precision=highest
        )

    slot_zero = jnp.zeros((total_slots, size_block, feat_width), jnp.float32)
    slot_grads = lax.fori_loop(0, steps_live, backward_step, slot_zero)
    incoming, slot_grads = lax.optimization_barrier((incoming, slot_grads))

    returned = lax.all_to_all(
        slot_grads.astype(SLOT_GRAD_LINK_DTYPE).reshape(
            row_devices, slots_peer * size_block, feat_width
        ),
        "rows",
        split_axis=0,
        concat_axis=0,
        tiled=True,
    )

    received = incoming.reshape(total_slots, size_block, feat_width)

    def forward_step(block_index, running):
        first_tile = block_index * step_tiles
        sources = received[src_ids]
        messages = jnp.einsum(
            "tij,tjf->tif", adjacency, sources, preferred_element_type=jnp.float32
        )
        weights = tile_weights(first_tile)
        return running + lax.dot_general(
            weights, messages, contract_first, precision=highest
        )

    zero_total = jnp.zeros((local_blocks * num_bases, size_block, feat_width), jnp.float32)
    partial_value = lax.fori_loop(0, steps_live, forward_step, zero_total)
    partial_value = partial_value.reshape(local_blocks, num_bases, size_block, feat_width)
    basis_f32 = bases.astype(jnp.float32)
    cot_f32 = cot_blocks.astype(jnp.float32)
    root_term = jnp.dot(features, root, preferred_element_type=jnp.float32)
    root_local = lax.dot_general(
        features, cotangent, contract_first, preferred_element_type=jnp.float32
    )
    projected_part = jnp.einsum("lbnf,bfg->lng", partial_value, basis_f32, precision=highest)
    basis_local = jnp.einsum("lbnf,lng->bfg", partial_value, cot_f32, precision=highest)
    root_grad = a2a_psum(root_local, ("rows",))
    returned, basis_local, projected_part = lax.optimization_barrier(
        (returned, basis_local, projected_part)
    )

    basis_grad = a2a_psum(
        basis_local.reshape(-1, basis_local.shape[-1]), ("rows", "rel")
    ).reshape(basis_local.shape)

    block_hot = (send_rows.reshape(-1)[None, :] == jnp.arange(local_blocks)[:, None]).astype(
        jnp.float32
    )
    own_grads = lax.dot_general(
        block_hot,
        returned.astype(jnp.float32).reshape(total_slots, size_block, feat_width),
        (((1,), (0,)), ((), ())),
        precision=highest,
    )
    both = jnp.concatenate(
        [projected_part.reshape(-1, feat_width), own_grads.reshape(-1, feat_width)]
    )
    summed_both = a2a_psum(both, ("rel",))
    projected = summed_both[: features.shape[0]]
    summed = summed_both[features.shape[0] :]
    output = (projected + root_term).astype(jnp.bfloat16)
    root_back = lax.dot_general(
        cotangent, root, (((1,), (1,)), ((), ())), preferred_element_type=jnp.float32
    )
    feature_grad = summed.reshape(-1, feat_width) + root_back
    return (output, feature_grad, basis_grad, root_grad)


def solution(mesh):
    return jax.shard_map(
        on_device,
        mesh=mesh,
        in_specs=(
            P("rows", None),
            P(),
            P(),
            P("rel", None),
            P("rows", "rel", None, None, None),
            P("rows", "rel", None),
            P("rows", "rel", None),
            P("rows", "rel", None),
            P("rows", "rel"),
            P("rows", "rel", None, None),
            P("rows", None),
        ),
        out_specs=(P("rows", None), P("rows", None), P(), P()),
        check_vma=False,
    )
```

```python
import math

import jax
import jax.numpy as jnp
from jax import lax
from jax.sharding import PartitionSpec as P

SLOT_GRAD_LINK_DTYPE = jnp.bfloat16


def a2a_psum(value, axes):
    count = 1
    for name in axes:
        count *= lax.axis_size(name)
    chunked = value.reshape((count, value.shape[0] // count) + value.shape[1:])
    pieces = lax.all_to_all(chunked, axes, 0, 0, tiled=True)
    reduced = jnp.sum(pieces, axis=0, keepdims=True)
    gathered = lax.all_to_all(jnp.broadcast_to(reduced, chunked.shape), axes, 0, 0, tiled=True)
    return gathered.reshape(value.shape)


def split_hi_lo(value):
    high = value.astype(jnp.bfloat16)
    low = (value - high.astype(jnp.float32)).astype(jnp.bfloat16)
    return jnp.concatenate([high, low], axis=1)


def join_hi_lo(pair):
    half = pair.shape[1] // 2
    return pair[:, :half].astype(jnp.float32) + pair[:, half:].astype(jnp.float32)


def on_device(
    features,
    bases,
    root,
    coeffs,
    tiles,
    tile_dst,
    tile_src,
    tile_rel,
    tile_live,
    send_list,
    cotangent,
):
    highest = lax.Precision.HIGHEST
    contract_first = (((0,), (0,)), ((), ()))
    feat_width = features.shape[1]
    size_block = tiles.shape[-1]
    blocks = features.reshape(-1, size_block, feat_width)
    local_blocks = blocks.shape[0]
    num_bases = bases.shape[0]
    slots_peer = send_list.shape[-1]
    row_devices = lax.axis_size("rows")
    total_slots = row_devices * slots_peer
    count_tiles = tiles.shape[2]
    adjacency = tiles[0, 0]
    dst_ids = tile_dst[0, 0]
    src_ids = tile_src[0, 0]
    rel_ids = tile_rel[0, 0]
    live_count = tile_live[0, 0]
    send_rows = send_list[0, 0]
    step_tiles = math.gcd(count_tiles, 64)
    steps_live = (live_count + step_tiles - 1) // step_tiles

    def tile_weights(first_tile):
        position = first_tile + jnp.arange(step_tiles)
        in_use = (position < live_count).astype(jnp.float32)
        rel_hot = (rel_ids[:, None] == jnp.arange(coeffs.shape[0])[None, :]).astype(jnp.float32)
        coef_rows = jnp.dot(rel_hot, coeffs, precision=highest)
        dst_hot = (dst_ids[:, None] == jnp.arange(local_blocks)[None, :]).astype(
            jnp.float32
        ) * in_use[:, None]
        return (dst_hot[:, :, None] * coef_rows[:, None, :]).reshape(
            step_tiles, local_blocks * num_bases
        )

    root_local = lax.dot_general(
        features, cotangent, contract_first, preferred_element_type=jnp.float32
    )
    root_rows = root_local.shape[0] // row_devices
    root_chunks = root_local.reshape(row_devices, root_rows, feat_width)
    outgoing = blocks[send_rows].reshape(row_devices, slots_peer * size_block, feat_width)
    outgoing = jnp.concatenate([outgoing, split_hi_lo(root_chunks)], axis=1)
    incoming = lax.all_to_all(outgoing, "rows", split_axis=0, concat_axis=0, tiled=True)
    block_rows = slots_peer * size_block
    root_mine = jnp.sum(join_hi_lo(incoming[:, block_rows:]), axis=0, keepdims=True)
    incoming = incoming[:, :block_rows]

    cot_blocks = cotangent.reshape(local_blocks, size_block, feat_width)
    agg_grad = jnp.einsum("lng,bfg->lbnf", cot_blocks, bases, preferred_element_type=jnp.float32)
    agg_grad = agg_grad.reshape(local_blocks * num_bases, size_block, feat_width)

    def backward_step(block_index, running):
        first_tile = block_index * step_tiles
        weights = tile_weights(first_tile)
        spread = lax.dot_general(
            weights, agg_grad, (((1,), (0,)), ((), ())), precision=highest
        ).astype(jnp.bfloat16)
        backward_term = jnp.einsum(
            "tij,tif->tjf", adjacency, spread, preferred_element_type=jnp.float32
        )
        slot_hot = (src_ids[:, None] == jnp.arange(total_slots)[None, :]).astype(jnp.float32)
        return running + lax.dot_general(
            slot_hot, backward_term, contract_first, precision=highest
        )

    slot_zero = jnp.zeros((total_slots, size_block, feat_width), jnp.float32)
    slot_grads = lax.fori_loop(0, steps_live, backward_step, slot_zero)
    incoming, slot_grads, root_mine = lax.optimization_barrier((incoming, slot_grads, root_mine))

    slot_out = slot_grads.astype(SLOT_GRAD_LINK_DTYPE).reshape(
        row_devices, slots_peer * size_block, feat_width
    )
    root_bcast = jnp.broadcast_to(root_mine, (row_devices,) + root_mine.shape[1:])
    slot_out = jnp.concatenate([slot_out, split_hi_lo(root_bcast)], axis=1)
    returned = lax.all_to_all(slot_out, "rows", split_axis=0, concat_axis=0, tiled=True)
    root_grad = join_hi_lo(returned[:, block_rows:]).reshape(root_local.shape)
    returned = returned[:, :block_rows]

    received = incoming.reshape(total_slots, size_block, feat_width)

    def forward_step(block_index, running):
        first_tile = block_index * step_tiles
        sources = received[src_ids]
        messages = jnp.einsum(
            "tij,tjf->tif", adjacency, sources, preferred_element_type=jnp.float32
        )
        weights = tile_weights(first_tile)
        return running + lax.dot_general(
            weights, messages, contract_first, precision=highest
        )

    zero_total = jnp.zeros((local_blocks * num_bases, size_block, feat_width), jnp.float32)
    partial_value = lax.fori_loop(0, steps_live, forward_step, zero_total)
    partial_value = partial_value.reshape(local_blocks, num_bases, size_block, feat_width)
    basis_f32 = bases.astype(jnp.float32)
    cot_f32 = cot_blocks.astype(jnp.float32)
    root_term = jnp.dot(features, root, preferred_element_type=jnp.float32)
    projected_part = jnp.einsum("lbnf,bfg->lng", partial_value, basis_f32, precision=highest)
    basis_local = jnp.einsum("lbnf,lng->bfg", partial_value, cot_f32, precision=highest)
    returned, basis_local, projected_part = lax.optimization_barrier(
        (returned, basis_local, projected_part)
    )

    basis_grad = a2a_psum(
        basis_local.reshape(-1, basis_local.shape[-1]), ("rows", "rel")
    ).reshape(basis_local.shape)

    block_hot = (send_rows.reshape(-1)[None, :] == jnp.arange(local_blocks)[:, None]).astype(
        jnp.float32
    )
    own_grads = lax.dot_general(
        block_hot,
        returned.astype(jnp.float32).reshape(total_slots, size_block, feat_width),
        (((1,), (0,)), ((), ())),
        precision=highest,
    )
    both = jnp.concatenate(
        [projected_part.reshape(-1, feat_width), own_grads.reshape(-1, feat_width)]
    )
    summed_both = a2a_psum(both, ("rel",))
    projected = summed_both[: features.shape[0]]
    summed = summed_both[features.shape[0] :]
    output = (projected + root_term).astype(jnp.bfloat16)
    root_back = lax.dot_general(
        cotangent, root, (((1,), (1,)), ((), ())), preferred_element_type=jnp.float32
    )
    feature_grad = summed.reshape(-1, feat_width) + root_back
    return (output, feature_grad, basis_grad, root_grad)


def solution(mesh):
    return jax.shard_map(
        on_device,
        mesh=mesh,
        in_specs=(
            P("rows", None),
            P(),
            P(),
            P("rel", None),
            P("rows", "rel", None, None, None),
            P("rows", "rel", None),
            P("rows", "rel", None),
            P("rows", "rel", None),
            P("rows", "rel"),
            P("rows", "rel", None, None),
            P("rows", None),
        ),
        out_specs=(P("rows", None), P("rows", None), P(), P()),
        check_vma=False,
    )
```

```python
import math

import jax
import jax.numpy as jnp
from jax import lax
from jax.sharding import PartitionSpec as P

SLOT_GRAD_LINK_DTYPE = jnp.bfloat16


def a2a_psum(value, axes):
    count = 1
    for name in axes:
        count *= lax.axis_size(name)
    chunked = value.reshape((count, value.shape[0] // count) + value.shape[1:])
    pieces = lax.all_to_all(chunked, axes, 0, 0, tiled=True)
    reduced = jnp.sum(pieces, axis=0, keepdims=True)
    gathered = lax.all_to_all(jnp.broadcast_to(reduced, chunked.shape), axes, 0, 0, tiled=True)
    return gathered.reshape(value.shape)


def split_hi_lo(value):
    high = lax.optimization_barrier(value.astype(jnp.bfloat16))
    low = (value - high.astype(jnp.float32)).astype(jnp.bfloat16)
    return jnp.concatenate([high, low], axis=1)


def join_hi_lo(pair):
    half = pair.shape[1] // 2
    return pair[:, :half].astype(jnp.float32) + pair[:, half:].astype(jnp.float32)


def on_device(
    features,
    bases,
    root,
    coeffs,
    tiles,
    tile_dst,
    tile_src,
    tile_rel,
    tile_live,
    send_list,
    cotangent,
):
    highest = lax.Precision.HIGHEST
    contract_first = (((0,), (0,)), ((), ()))
    feat_width = features.shape[1]
    size_block = tiles.shape[-1]
    blocks = features.reshape(-1, size_block, feat_width)
    local_blocks = blocks.shape[0]
    num_bases = bases.shape[0]
    slots_peer = send_list.shape[-1]
    row_devices = lax.axis_size("rows")
    total_slots = row_devices * slots_peer
    count_tiles = tiles.shape[2]
    adjacency = tiles[0, 0]
    dst_ids = tile_dst[0, 0]
    src_ids = tile_src[0, 0]
    rel_ids = tile_rel[0, 0]
    live_count = tile_live[0, 0]
    send_rows = send_list[0, 0]
    step_tiles = math.gcd(count_tiles, 64)
    steps_live = (live_count + step_tiles - 1) // step_tiles

    def tile_weights(first_tile):
        position = first_tile + jnp.arange(step_tiles)
        in_use = (position < live_count).astype(jnp.float32)
        rel_hot = (rel_ids[:, None] == jnp.arange(coeffs.shape[0])[None, :]).astype(jnp.float32)
        coef_rows = jnp.dot(rel_hot, coeffs, precision=highest)
        dst_hot = (dst_ids[:, None] == jnp.arange(local_blocks)[None, :]).astype(
            jnp.float32
        ) * in_use[:, None]
        return (dst_hot[:, :, None] * coef_rows[:, None, :]).reshape(
            step_tiles, local_blocks * num_bases
        )

    root_local = lax.dot_general(
        features, cotangent, contract_first, preferred_element_type=jnp.float32
    )
    root_rows = root_local.shape[0] // row_devices
    root_chunks = root_local.reshape(row_devices, root_rows, feat_width)
    outgoing = blocks[send_rows].reshape(row_devices, slots_peer * size_block, feat_width)
    outgoing = jnp.concatenate([outgoing, split_hi_lo(root_chunks)], axis=1)
    incoming = lax.all_to_all(outgoing, "rows", split_axis=0, concat_axis=0, tiled=True)
    block_rows = slots_peer * size_block
    root_mine = jnp.sum(join_hi_lo(incoming[:, block_rows:]), axis=0, keepdims=True)
    incoming = incoming[:, :block_rows]

    cot_blocks = cotangent.reshape(local_blocks, size_block, feat_width)
    agg_grad = jnp.einsum("lng,bfg->lbnf", cot_blocks, bases, preferred_element_type=jnp.float32)
    agg_grad = agg_grad.reshape(local_blocks * num_bases, size_block, feat_width)

    def backward_step(block_index, running):
        first_tile = block_index * step_tiles
        weights = tile_weights(first_tile)
        spread = lax.dot_general(
            weights, agg_grad, (((1,), (0,)), ((), ())), precision=highest
        ).astype(jnp.bfloat16)
        backward_term = jnp.einsum(
            "tij,tif->tjf", adjacency, spread, preferred_element_type=jnp.float32
        )
        slot_hot = (src_ids[:, None] == jnp.arange(total_slots)[None, :]).astype(jnp.float32)
        return running + lax.dot_general(
            slot_hot, backward_term, contract_first, precision=highest
        )

    slot_zero = jnp.zeros((total_slots, size_block, feat_width), jnp.float32)
    slot_grads = lax.fori_loop(0, steps_live, backward_step, slot_zero)
    incoming, slot_grads, root_mine = lax.optimization_barrier((incoming, slot_grads, root_mine))

    slot_out = slot_grads.astype(SLOT_GRAD_LINK_DTYPE).reshape(
        row_devices, slots_peer * size_block, feat_width
    )
    root_bcast = jnp.broadcast_to(root_mine, (row_devices,) + root_mine.shape[1:])
    slot_out = jnp.concatenate([slot_out, split_hi_lo(root_bcast)], axis=1)
    returned = lax.all_to_all(slot_out, "rows", split_axis=0, concat_axis=0, tiled=True)
    root_grad = join_hi_lo(returned[:, block_rows:]).reshape(root_local.shape)
    returned = returned[:, :block_rows]

    received = incoming.reshape(total_slots, size_block, feat_width)

    def forward_step(block_index, running):
        first_tile = block_index * step_tiles
        sources = received[src_ids]
        messages = jnp.einsum(
            "tij,tjf->tif", adjacency, sources, preferred_element_type=jnp.float32
        )
        weights = tile_weights(first_tile)
        return running + lax.dot_general(
            weights, messages, contract_first, precision=highest
        )

    zero_total = jnp.zeros((local_blocks * num_bases, size_block, feat_width), jnp.float32)
    partial_value = lax.fori_loop(0, steps_live, forward_step, zero_total)
    partial_value = partial_value.reshape(local_blocks, num_bases, size_block, feat_width)
    basis_f32 = bases.astype(jnp.float32)
    cot_f32 = cot_blocks.astype(jnp.float32)
    root_term = jnp.dot(features, root, preferred_element_type=jnp.float32)
    projected_part = jnp.einsum("lbnf,bfg->lng", partial_value, basis_f32, precision=highest)
    basis_local = jnp.einsum("lbnf,lng->bfg", partial_value, cot_f32, precision=highest)
    returned, basis_local, projected_part = lax.optimization_barrier(
        (returned, basis_local, projected_part)
    )

    basis_grad = a2a_psum(
        basis_local.reshape(-1, basis_local.shape[-1]), ("rows", "rel")
    ).reshape(basis_local.shape)

    block_hot = (send_rows.reshape(-1)[None, :] == jnp.arange(local_blocks)[:, None]).astype(
        jnp.float32
    )
    own_grads = lax.dot_general(
        block_hot,
        returned.astype(jnp.float32).reshape(total_slots, size_block, feat_width),
        (((1,), (0,)), ((), ())),
        precision=highest,
    )
    both = jnp.concatenate(
        [projected_part.reshape(-1, feat_width), own_grads.reshape(-1, feat_width)]
    )
    summed_both = a2a_psum(both, ("rel",))
    projected = summed_both[: features.shape[0]]
    summed = summed_both[features.shape[0] :]
    output = (projected + root_term).astype(jnp.bfloat16)
    root_back = lax.dot_general(
        cotangent, root, (((1,), (1,)), ((), ())), preferred_element_type=jnp.float32
    )
    feature_grad = summed.reshape(-1, feat_width) + root_back
    return (output, feature_grad, basis_grad, root_grad)


def solution(mesh):
    return jax.shard_map(
        on_device,
        mesh=mesh,
        in_specs=(
            P("rows", None),
            P(),
            P(),
            P("rel", None),
            P("rows", "rel", None, None, None),
            P("rows", "rel", None),
            P("rows", "rel", None),
            P("rows", "rel", None),
            P("rows", "rel"),
            P("rows", "rel", None, None),
            P("rows", None),
        ),
        out_specs=(P("rows", None), P("rows", None), P(), P()),
        check_vma=False,
    )
```

```python
import math

import jax
import jax.numpy as jnp
from jax import lax
from jax.sharding import PartitionSpec as P

SLOT_GRAD_LINK_DTYPE = jnp.bfloat16


def a2a_psum(value, axes):
    count = 1
    for name in axes:
        count *= lax.axis_size(name)
    chunked = value.reshape((count, value.shape[0] // count) + value.shape[1:])
    pieces = lax.all_to_all(chunked, axes, 0, 0, tiled=True)
    reduced = jnp.sum(pieces, axis=0, keepdims=True)
    gathered = lax.all_to_all(jnp.broadcast_to(reduced, chunked.shape), axes, 0, 0, tiled=True)
    return gathered.reshape(value.shape)


def pair_psum(value):
    rows_n = lax.axis_size("rows")
    rel_n = lax.axis_size("rel")
    count = rows_n * rel_n
    swap = [(index, index ^ 1) for index in range(rows_n)]
    core = lax.axis_index("rows") % 2
    half = value.shape[0] // 2
    first, second = value[:half], value[half:]
    kept = jnp.where(core == 0, first, second)
    given = jnp.where(core == 0, second, first)
    chip_sum = kept + lax.ppermute(given, "rows", swap)
    pieces = lax.all_to_all(
        chip_sum.reshape((count, half // count) + value.shape[1:]), ("rows", "rel"), 0, 0, tiled=True
    )
    pieces = pieces.reshape((rows_n // 2, 2, rel_n, half // count) + value.shape[1:])
    reduced = jnp.sum(pieces, axis=(0, 2))
    outgoing = jnp.broadcast_to(reduced[None, :, None], pieces.shape).reshape(
        (count, half // count) + value.shape[1:]
    )
    own_half = lax.all_to_all(outgoing, ("rows", "rel"), 0, 0, tiled=True).reshape(
        (half,) + value.shape[1:]
    )
    other_half = lax.ppermute(own_half, "rows", swap)
    return jnp.where(
        core == 0,
        jnp.concatenate([own_half, other_half]),
        jnp.concatenate([other_half, own_half]),
    )


def split_hi_lo(value):
    high = lax.optimization_barrier(value.astype(jnp.bfloat16))
    low = (value - high.astype(jnp.float32)).astype(jnp.bfloat16)
    return jnp.concatenate([high, low], axis=1)


def join_hi_lo(pair):
    half = pair.shape[1] // 2
    return pair[:, :half].astype(jnp.float32) + pair[:, half:].astype(jnp.float32)


def on_device(
    features,
    bases,
    root,
    coeffs,
    tiles,
    tile_dst,
    tile_src,
    tile_rel,
    tile_live,
    send_list,
    cotangent,
):
    highest = lax.Precision.HIGHEST
    contract_first = (((0,), (0,)), ((), ()))
    feat_width = features.shape[1]
    size_block = tiles.shape[-1]
    blocks = features.reshape(-1, size_block, feat_width)
    local_blocks = blocks.shape[0]
    num_bases = bases.shape[0]
    slots_peer = send_list.shape[-1]
    row_devices = lax.axis_size("rows")
    total_slots = row_devices * slots_peer
    count_tiles = tiles.shape[2]
    adjacency = tiles[0, 0]
    dst_ids = tile_dst[0, 0]
    src_ids = tile_src[0, 0]
    rel_ids = tile_rel[0, 0]
    live_count = tile_live[0, 0]
    send_rows = send_list[0, 0]
    step_tiles = math.gcd(count_tiles, 64)
    steps_live = (live_count + step_tiles - 1) // step_tiles

    def tile_weights(first_tile):
        position = first_tile + jnp.arange(step_tiles)
        in_use = (position < live_count).astype(jnp.float32)
        rel_hot = (rel_ids[:, None] == jnp.arange(coeffs.shape[0])[None, :]).astype(jnp.float32)
        coef_rows = jnp.dot(rel_hot, coeffs, precision=highest)
        dst_hot = (dst_ids[:, None] == jnp.arange(local_blocks)[None, :]).astype(
            jnp.float32
        ) * in_use[:, None]
        return (dst_hot[:, :, None] * coef_rows[:, None, :]).reshape(
            step_tiles, local_blocks * num_bases
        )

    root_local = lax.dot_general(
        features, cotangent, contract_first, preferred_element_type=jnp.float32
    )
    root_rows = root_local.shape[0] // row_devices
    root_chunks = root_local.reshape(row_devices, root_rows, feat_width)
    outgoing = blocks[send_rows].reshape(row_devices, slots_peer * size_block, feat_width)
    outgoing = jnp.concatenate([outgoing, split_hi_lo(root_chunks)], axis=1)
    incoming = lax.all_to_all(outgoing, "rows", split_axis=0, concat_axis=0, tiled=True)
    block_rows = slots_peer * size_block
    root_mine = jnp.sum(join_hi_lo(incoming[:, block_rows:]), axis=0, keepdims=True)
    incoming = incoming[:, :block_rows]

    cot_blocks = cotangent.reshape(local_blocks, size_block, feat_width)
    agg_grad = jnp.einsum("lng,bfg->lbnf", cot_blocks, bases, preferred_element_type=jnp.float32)
    agg_grad = agg_grad.reshape(local_blocks * num_bases, size_block, feat_width)

    def backward_step(block_index, running):
        first_tile = block_index * step_tiles
        weights = tile_weights(first_tile)
        spread = lax.dot_general(
            weights, agg_grad, (((1,), (0,)), ((), ())), precision=highest
        ).astype(jnp.bfloat16)
        backward_term = jnp.einsum(
            "tij,tif->tjf", adjacency, spread, preferred_element_type=jnp.float32
        )
        slot_hot = (src_ids[:, None] == jnp.arange(total_slots)[None, :]).astype(jnp.float32)
        return running + lax.dot_general(
            slot_hot, backward_term, contract_first, precision=highest
        )

    slot_zero = jnp.zeros((total_slots, size_block, feat_width), jnp.float32)
    slot_grads = lax.fori_loop(0, steps_live, backward_step, slot_zero)
    incoming, slot_grads, root_mine = lax.optimization_barrier((incoming, slot_grads, root_mine))

    slot_out = slot_grads.astype(SLOT_GRAD_LINK_DTYPE).reshape(
        row_devices, slots_peer * size_block, feat_width
    )
    root_bcast = jnp.broadcast_to(root_mine, (row_devices,) + root_mine.shape[1:])
    slot_out = jnp.concatenate([slot_out, split_hi_lo(root_bcast)], axis=1)
    returned = lax.all_to_all(slot_out, "rows", split_axis=0, concat_axis=0, tiled=True)
    root_grad = join_hi_lo(returned[:, block_rows:]).reshape(root_local.shape)
    returned = returned[:, :block_rows]

    received = incoming.reshape(total_slots, size_block, feat_width)

    def forward_step(block_index, running):
        first_tile = block_index * step_tiles
        sources = received[src_ids]
        messages = jnp.einsum(
            "tij,tjf->tif", adjacency, sources, preferred_element_type=jnp.float32
        )
        weights = tile_weights(first_tile)
        return running + lax.dot_general(
            weights, messages, contract_first, precision=highest
        )

    zero_total = jnp.zeros((local_blocks * num_bases, size_block, feat_width), jnp.float32)
    partial_value = lax.fori_loop(0, steps_live, forward_step, zero_total)
    partial_value = partial_value.reshape(local_blocks, num_bases, size_block, feat_width)
    basis_f32 = bases.astype(jnp.float32)
    cot_f32 = cot_blocks.astype(jnp.float32)
    root_term = jnp.dot(features, root, preferred_element_type=jnp.float32)
    projected_part = jnp.einsum("lbnf,bfg->lng", partial_value, basis_f32, precision=highest)
    basis_local = jnp.einsum("lbnf,lng->bfg", partial_value, cot_f32, precision=highest)
    returned, basis_local, projected_part = lax.optimization_barrier(
        (returned, basis_local, projected_part)
    )

    basis_grad = pair_psum(basis_local.reshape(-1, basis_local.shape[-1])).reshape(
        basis_local.shape
    )

    block_hot = (send_rows.reshape(-1)[None, :] == jnp.arange(local_blocks)[:, None]).astype(
        jnp.float32
    )
    own_grads = lax.dot_general(
        block_hot,
        returned.astype(jnp.float32).reshape(total_slots, size_block, feat_width),
        (((1,), (0,)), ((), ())),
        precision=highest,
    )
    both = jnp.concatenate(
        [projected_part.reshape(-1, feat_width), own_grads.reshape(-1, feat_width)]
    )
    summed_both = a2a_psum(both, ("rel",))
    projected = summed_both[: features.shape[0]]
    summed = summed_both[features.shape[0] :]
    output = (projected + root_term).astype(jnp.bfloat16)
    root_back = lax.dot_general(
        cotangent, root, (((1,), (1,)), ((), ())), preferred_element_type=jnp.float32
    )
    feature_grad = summed.reshape(-1, feat_width) + root_back
    return (output, feature_grad, basis_grad, root_grad)


def solution(mesh):
    return jax.shard_map(
        on_device,
        mesh=mesh,
        in_specs=(
            P("rows", None),
            P(),
            P(),
            P("rel", None),
            P("rows", "rel", None, None, None),
            P("rows", "rel", None),
            P("rows", "rel", None),
            P("rows", "rel", None),
            P("rows", "rel"),
            P("rows", "rel", None, None),
            P("rows", None),
        ),
        out_specs=(P("rows", None), P("rows", None), P(), P()),
        check_vma=False,
    )
```

```python
import math

import jax
import jax.numpy as jnp
from jax import lax
from jax.sharding import PartitionSpec as P

SLOT_GRAD_LINK_DTYPE = jnp.bfloat16


def a2a_psum(value, axes):
    count = 1
    for name in axes:
        count *= lax.axis_size(name)
    chunked = value.reshape((count, value.shape[0] // count) + value.shape[1:])
    pieces = lax.all_to_all(chunked, axes, 0, 0, tiled=True)
    reduced = jnp.sum(pieces, axis=0, keepdims=True)
    gathered = lax.all_to_all(jnp.broadcast_to(reduced, chunked.shape), axes, 0, 0, tiled=True)
    return gathered.reshape(value.shape)


def pair_psum(value):
    rows_n = lax.axis_size("rows")
    rel_n = lax.axis_size("rel")
    count = rows_n * rel_n
    swap = [(index, index ^ 1) for index in range(rows_n)]
    core = lax.axis_index("rows") % 2
    half = value.shape[0] // 2
    first, second = value[:half], value[half:]
    kept = jnp.where(core == 0, first, second)
    given = jnp.where(core == 0, second, first)
    chip_sum = kept + lax.ppermute(given, "rows", swap)
    pieces = lax.all_to_all(
        chip_sum.reshape((count, half // count) + value.shape[1:]), ("rows", "rel"), 0, 0, tiled=True
    )
    pieces = pieces.reshape((rows_n // 2, 2, rel_n, half // count) + value.shape[1:])
    reduced = jnp.sum(pieces, axis=(0, 2))
    outgoing = jnp.broadcast_to(reduced[None, :, None], pieces.shape).reshape(
        (count, half // count) + value.shape[1:]
    )
    own_half = lax.all_to_all(outgoing, ("rows", "rel"), 0, 0, tiled=True).reshape(
        (half,) + value.shape[1:]
    )
    other_half = lax.ppermute(own_half, "rows", swap)
    return jnp.where(
        core == 0,
        jnp.concatenate([own_half, other_half]),
        jnp.concatenate([other_half, own_half]),
    )


def permute_psum(value, axis):
    size = lax.axis_size(axis)
    me = lax.axis_index(axis)
    chunks = value.reshape((size, value.shape[0] // size) + value.shape[1:])
    total = chunks[me]
    for shift in range(1, size):
        pairs = [(index, (index + shift) % size) for index in range(size)]
        total = total + lax.ppermute(chunks[(me + shift) % size], axis, pairs)
    parts = [total]
    for shift in range(1, size):
        pairs = [(index, (index + shift) % size) for index in range(size)]
        parts.append(lax.ppermute(total, axis, pairs))
    stacked = jnp.stack(parts)
    order = (me - jnp.arange(size)) % size
    return stacked[order].reshape(value.shape)


def split_hi_lo(value):
    high = lax.optimization_barrier(value.astype(jnp.bfloat16))
    low = (value - high.astype(jnp.float32)).astype(jnp.bfloat16)
    return jnp.concatenate([high, low], axis=1)


def join_hi_lo(pair):
    half = pair.shape[1] // 2
    return pair[:, :half].astype(jnp.float32) + pair[:, half:].astype(jnp.float32)


def on_device(
    features,
    bases,
    root,
    coeffs,
    tiles,
    tile_dst,
    tile_src,
    tile_rel,
    tile_live,
    send_list,
    cotangent,
):
    highest = lax.Precision.HIGHEST
    contract_first = (((0,), (0,)), ((), ()))
    feat_width = features.shape[1]
    size_block = tiles.shape[-1]
    blocks = features.reshape(-1, size_block, feat_width)
    local_blocks = blocks.shape[0]
    num_bases = bases.shape[0]
    slots_peer = send_list.shape[-1]
    row_devices = lax.axis_size("rows")
    total_slots = row_devices * slots_peer
    count_tiles = tiles.shape[2]
    adjacency = tiles[0, 0]
    dst_ids = tile_dst[0, 0]
    src_ids = tile_src[0, 0]
    rel_ids = tile_rel[0, 0]
    live_count = tile_live[0, 0]
    send_rows = send_list[0, 0]
    step_tiles = math.gcd(count_tiles, 64)
    steps_live = (live_count + step_tiles - 1) // step_tiles

    def tile_weights(first_tile):
        position = first_tile + jnp.arange(step_tiles)
        in_use = (position < live_count).astype(jnp.float32)
        rel_hot = (rel_ids[:, None] == jnp.arange(coeffs.shape[0])[None, :]).astype(jnp.float32)
        coef_rows = jnp.dot(rel_hot, coeffs, precision=highest)
        dst_hot = (dst_ids[:, None] == jnp.arange(local_blocks)[None, :]).astype(
            jnp.float32
        ) * in_use[:, None]
        return (dst_hot[:, :, None] * coef_rows[:, None, :]).reshape(
            step_tiles, local_blocks * num_bases
        )

    root_local = lax.dot_general(
        features, cotangent, contract_first, preferred_element_type=jnp.float32
    )
    root_rows = root_local.shape[0] // row_devices
    root_chunks = root_local.reshape(row_devices, root_rows, feat_width)
    outgoing = blocks[send_rows].reshape(row_devices, slots_peer * size_block, feat_width)
    outgoing = jnp.concatenate([outgoing, split_hi_lo(root_chunks)], axis=1)
    incoming = lax.all_to_all(outgoing, "rows", split_axis=0, concat_axis=0, tiled=True)
    block_rows = slots_peer * size_block
    root_mine = jnp.sum(join_hi_lo(incoming[:, block_rows:]), axis=0, keepdims=True)
    incoming = incoming[:, :block_rows]

    cot_blocks = cotangent.reshape(local_blocks, size_block, feat_width)
    agg_grad = jnp.einsum("lng,bfg->lbnf", cot_blocks, bases, preferred_element_type=jnp.float32)
    agg_grad = agg_grad.reshape(local_blocks * num_bases, size_block, feat_width)

    def backward_step(block_index, running):
        first_tile = block_index * step_tiles
        weights = tile_weights(first_tile)
        spread = lax.dot_general(
            weights, agg_grad, (((1,), (0,)), ((), ())), precision=highest
        ).astype(jnp.bfloat16)
        backward_term = jnp.einsum(
            "tij,tif->tjf", adjacency, spread, preferred_element_type=jnp.float32
        )
        slot_hot = (src_ids[:, None] == jnp.arange(total_slots)[None, :]).astype(jnp.float32)
        return running + lax.dot_general(
            slot_hot, backward_term, contract_first, precision=highest
        )

    slot_zero = jnp.zeros((total_slots, size_block, feat_width), jnp.float32)
    slot_grads = lax.fori_loop(0, steps_live, backward_step, slot_zero)
    incoming, slot_grads, root_mine = lax.optimization_barrier((incoming, slot_grads, root_mine))

    slot_out = slot_grads.astype(SLOT_GRAD_LINK_DTYPE).reshape(
        row_devices, slots_peer * size_block, feat_width
    )
    root_bcast = jnp.broadcast_to(root_mine, (row_devices,) + root_mine.shape[1:])
    slot_out = jnp.concatenate([slot_out, split_hi_lo(root_bcast)], axis=1)
    returned = lax.all_to_all(slot_out, "rows", split_axis=0, concat_axis=0, tiled=True)
    root_grad = join_hi_lo(returned[:, block_rows:]).reshape(root_local.shape)
    returned = returned[:, :block_rows]

    received = incoming.reshape(total_slots, size_block, feat_width)

    def forward_step(block_index, running):
        first_tile = block_index * step_tiles
        sources = received[src_ids]
        messages = jnp.einsum(
            "tij,tjf->tif", adjacency, sources, preferred_element_type=jnp.float32
        )
        weights = tile_weights(first_tile)
        return running + lax.dot_general(
            weights, messages, contract_first, precision=highest
        )

    zero_total = jnp.zeros((local_blocks * num_bases, size_block, feat_width), jnp.float32)
    partial_value = lax.fori_loop(0, steps_live, forward_step, zero_total)
    partial_value = partial_value.reshape(local_blocks, num_bases, size_block, feat_width)
    basis_f32 = bases.astype(jnp.float32)
    cot_f32 = cot_blocks.astype(jnp.float32)
    root_term = jnp.dot(features, root, preferred_element_type=jnp.float32)
    projected_part = jnp.einsum("lbnf,bfg->lng", partial_value, basis_f32, precision=highest)
    basis_local = jnp.einsum("lbnf,lng->bfg", partial_value, cot_f32, precision=highest)
    returned, basis_local, projected_part = lax.optimization_barrier(
        (returned, basis_local, projected_part)
    )

    basis_grad = pair_psum(basis_local.reshape(-1, basis_local.shape[-1])).reshape(
        basis_local.shape
    )

    block_hot = (send_rows.reshape(-1)[None, :] == jnp.arange(local_blocks)[:, None]).astype(
        jnp.float32
    )
    own_grads = lax.dot_general(
        block_hot,
        returned.astype(jnp.float32).reshape(total_slots, size_block, feat_width),
        (((1,), (0,)), ((), ())),
        precision=highest,
    )
    both = jnp.concatenate(
        [projected_part.reshape(-1, feat_width), own_grads.reshape(-1, feat_width)]
    )
    summed_both = permute_psum(both, "rel")
    projected = summed_both[: features.shape[0]]
    summed = summed_both[features.shape[0] :]
    output = (projected + root_term).astype(jnp.bfloat16)
    root_back = lax.dot_general(
        cotangent, root, (((1,), (1,)), ((), ())), preferred_element_type=jnp.float32
    )
    feature_grad = summed.reshape(-1, feat_width) + root_back
    return (output, feature_grad, basis_grad, root_grad)


def solution(mesh):
    return jax.shard_map(
        on_device,
        mesh=mesh,
        in_specs=(
            P("rows", None),
            P(),
            P(),
            P("rel", None),
            P("rows", "rel", None, None, None),
            P("rows", "rel", None),
            P("rows", "rel", None),
            P("rows", "rel", None),
            P("rows", "rel"),
            P("rows", "rel", None, None),
            P("rows", None),
        ),
        out_specs=(P("rows", None), P("rows", None), P(), P()),
        check_vma=False,
    )
```

```python
import math

import jax
import jax.numpy as jnp
from jax import lax
from jax.sharding import PartitionSpec as P

SLOT_GRAD_LINK_DTYPE = jnp.bfloat16


def a2a_psum(value, axes):
    count = 1
    for name in axes:
        count *= lax.axis_size(name)
    chunked = value.reshape((count, value.shape[0] // count) + value.shape[1:])
    pieces = lax.all_to_all(chunked, axes, 0, 0, tiled=True)
    reduced = jnp.sum(pieces, axis=0, keepdims=True)
    gathered = lax.all_to_all(jnp.broadcast_to(reduced, chunked.shape), axes, 0, 0, tiled=True)
    return gathered.reshape(value.shape)


def pair_psum(value):
    rows_n = lax.axis_size("rows")
    rel_n = lax.axis_size("rel")
    count = rows_n * rel_n
    swap = [(index, index ^ 1) for index in range(rows_n)]
    core = lax.axis_index("rows") % 2
    half = value.shape[0] // 2
    first, second = value[:half], value[half:]
    kept = jnp.where(core == 0, first, second)
    given = jnp.where(core == 0, second, first)
    chip_sum = kept + lax.ppermute(given, "rows", swap)
    pieces = lax.all_to_all(
        chip_sum.reshape((count, half // count) + value.shape[1:]), ("rows", "rel"), 0, 0, tiled=True
    )
    pieces = pieces.reshape((rows_n // 2, 2, rel_n, half // count) + value.shape[1:])
    reduced = jnp.sum(pieces, axis=(0, 2))
    outgoing = jnp.broadcast_to(reduced[None, :, None], pieces.shape).reshape(
        (count, half // count) + value.shape[1:]
    )
    own_half = lax.all_to_all(outgoing, ("rows", "rel"), 0, 0, tiled=True).reshape(
        (half,) + value.shape[1:]
    )
    other_half = lax.ppermute(own_half, "rows", swap)
    return jnp.where(
        core == 0,
        jnp.concatenate([own_half, other_half]),
        jnp.concatenate([other_half, own_half]),
    )


def permute_psum(value, axis):
    size = lax.axis_size(axis)
    me = lax.axis_index(axis)
    chunks = value.reshape((size, value.shape[0] // size) + value.shape[1:])
    total = chunks[me]
    for shift in range(1, size):
        pairs = [(index, (index + shift) % size) for index in range(size)]
        total = total + lax.ppermute(chunks[(me + shift) % size], axis, pairs)
    parts = [total]
    for shift in range(1, size):
        pairs = [(index, (index + shift) % size) for index in range(size)]
        parts.append(lax.ppermute(total, axis, pairs))
    stacked = jnp.stack(parts)
    order = (me - jnp.arange(size)) % size
    return stacked[order].reshape(value.shape)


def split_hi_lo(value):
    high = lax.optimization_barrier(value.astype(jnp.bfloat16))
    low = (value - high.astype(jnp.float32)).astype(jnp.bfloat16)
    return jnp.concatenate([high, low], axis=1)


def join_hi_lo(pair):
    half = pair.shape[1] // 2
    return pair[:, :half].astype(jnp.float32) + pair[:, half:].astype(jnp.float32)


def on_device(
    features,
    bases,
    root,
    coeffs,
    tiles,
    tile_dst,
    tile_src,
    tile_rel,
    tile_live,
    send_list,
    cotangent,
):
    highest = lax.Precision.HIGHEST
    contract_first = (((0,), (0,)), ((), ()))
    feat_width = features.shape[1]
    size_block = tiles.shape[-1]
    blocks = features.reshape(-1, size_block, feat_width)
    local_blocks = blocks.shape[0]
    num_bases = bases.shape[0]
    slots_peer = send_list.shape[-1]
    row_devices = lax.axis_size("rows")
    total_slots = row_devices * slots_peer
    count_tiles = tiles.shape[2]
    adjacency = tiles[0, 0]
    dst_ids = tile_dst[0, 0]
    src_ids = tile_src[0, 0]
    rel_ids = tile_rel[0, 0]
    live_count = tile_live[0, 0]
    send_rows = send_list[0, 0]
    step_tiles = math.gcd(count_tiles, 64)
    steps_live = (live_count + step_tiles - 1) // step_tiles

    def tile_weights(first_tile):
        position = first_tile + jnp.arange(step_tiles)
        in_use = (position < live_count).astype(jnp.float32)
        rel_hot = (rel_ids[:, None] == jnp.arange(coeffs.shape[0])[None, :]).astype(jnp.float32)
        coef_rows = jnp.dot(rel_hot, coeffs, precision=highest)
        dst_hot = (dst_ids[:, None] == jnp.arange(local_blocks)[None, :]).astype(
            jnp.float32
        ) * in_use[:, None]
        return (dst_hot[:, :, None] * coef_rows[:, None, :]).reshape(
            step_tiles, local_blocks * num_bases
        )

    root_local = lax.dot_general(
        features, cotangent, contract_first, preferred_element_type=jnp.float32
    )
    root_rows = root_local.shape[0] // row_devices
    root_chunks = root_local.reshape(row_devices, root_rows, feat_width)
    outgoing = blocks[send_rows].reshape(row_devices, slots_peer * size_block, feat_width)
    outgoing = jnp.concatenate([outgoing, split_hi_lo(root_chunks)], axis=1)
    incoming = lax.all_to_all(outgoing, "rows", split_axis=0, concat_axis=0, tiled=True)
    block_rows = slots_peer * size_block
    root_mine = jnp.sum(join_hi_lo(incoming[:, block_rows:]), axis=0, keepdims=True)

    cot_blocks = cotangent.reshape(local_blocks, size_block, feat_width)
    agg_grad = jnp.einsum("lng,bfg->lbnf", cot_blocks, bases, preferred_element_type=jnp.float32)
    agg_grad = agg_grad.reshape(local_blocks * num_bases, size_block, feat_width)

    def backward_step(block_index, running):
        first_tile = block_index * step_tiles
        weights = tile_weights(first_tile)
        spread = lax.dot_general(
            weights, agg_grad, (((1,), (0,)), ((), ())), precision=highest
        ).astype(jnp.bfloat16)
        backward_term = jnp.einsum(
            "tij,tif->tjf", adjacency, spread, preferred_element_type=jnp.float32
        )
        slot_hot = (src_ids[:, None] == jnp.arange(total_slots)[None, :]).astype(jnp.float32)
        return running + lax.dot_general(
            slot_hot, backward_term, contract_first, precision=highest
        )

    slot_zero = jnp.zeros((total_slots, size_block, feat_width), jnp.float32)
    slot_grads = lax.fori_loop(0, steps_live, backward_step, slot_zero)
    incoming, slot_grads, root_mine = lax.optimization_barrier((incoming, slot_grads, root_mine))

    slot_out = slot_grads.astype(SLOT_GRAD_LINK_DTYPE).reshape(
        row_devices, slots_peer * size_block, feat_width
    )
    root_bcast = jnp.broadcast_to(root_mine, (row_devices,) + root_mine.shape[1:])
    slot_out = jnp.concatenate([slot_out, split_hi_lo(root_bcast)], axis=1)
    returned = lax.all_to_all(slot_out, "rows", split_axis=0, concat_axis=0, tiled=True)
    root_grad = join_hi_lo(returned[:, block_rows:]).reshape(root_local.shape)

    received = incoming[:, :block_rows].reshape(total_slots, size_block, feat_width)

    def forward_step(block_index, running):
        first_tile = block_index * step_tiles
        sources = received[src_ids]
        messages = jnp.einsum(
            "tij,tjf->tif", adjacency, sources, preferred_element_type=jnp.float32
        )
        weights = tile_weights(first_tile)
        return running + lax.dot_general(
            weights, messages, contract_first, precision=highest
        )

    zero_total = jnp.zeros((local_blocks * num_bases, size_block, feat_width), jnp.float32)
    partial_value = lax.fori_loop(0, steps_live, forward_step, zero_total)
    partial_value = partial_value.reshape(local_blocks, num_bases, size_block, feat_width)
    basis_f32 = bases.astype(jnp.float32)
    cot_f32 = cot_blocks.astype(jnp.float32)
    root_term = jnp.dot(features, root, preferred_element_type=jnp.float32)
    projected_part = jnp.einsum("lbnf,bfg->lng", partial_value, basis_f32, precision=highest)
    basis_local = jnp.einsum("lbnf,lng->bfg", partial_value, cot_f32, precision=highest)
    returned, basis_local, projected_part = lax.optimization_barrier(
        (returned, basis_local, projected_part)
    )

    basis_grad = pair_psum(basis_local.reshape(-1, basis_local.shape[-1])).reshape(
        basis_local.shape
    )

    block_hot = (send_rows.reshape(-1)[None, :] == jnp.arange(local_blocks)[:, None]).astype(
        jnp.float32
    )
    own_grads = lax.dot_general(
        block_hot,
        returned[:, :block_rows].astype(jnp.float32).reshape(total_slots, size_block, feat_width),
        (((1,), (0,)), ((), ())),
        precision=highest,
    )
    both = jnp.concatenate(
        [projected_part.reshape(-1, feat_width), own_grads.reshape(-1, feat_width)]
    )
    summed_both = permute_psum(both, "rel")
    projected = summed_both[: features.shape[0]]
    summed = summed_both[features.shape[0] :]
    output = (projected + root_term).astype(jnp.bfloat16)
    root_back = lax.dot_general(
        cotangent, root, (((1,), (1,)), ((), ())), preferred_element_type=jnp.float32
    )
    feature_grad = summed.reshape(-1, feat_width) + root_back
    return (output, feature_grad, basis_grad, root_grad)


def solution(mesh):
    return jax.shard_map(
        on_device,
        mesh=mesh,
        in_specs=(
            P("rows", None),
            P(),
            P(),
            P("rel", None),
            P("rows", "rel", None, None, None),
            P("rows", "rel", None),
            P("rows", "rel", None),
            P("rows", "rel", None),
            P("rows", "rel"),
            P("rows", "rel", None, None),
            P("rows", None),
        ),
        out_specs=(P("rows", None), P("rows", None), P(), P()),
        check_vma=False,
    )
```

```python
import math

import jax
import jax.numpy as jnp
from jax import lax
from jax.sharding import PartitionSpec as P

SLOT_GRAD_LINK_DTYPE = jnp.bfloat16


def a2a_psum(value, axes):
    count = 1
    for name in axes:
        count *= lax.axis_size(name)
    chunked = value.reshape((count, value.shape[0] // count) + value.shape[1:])
    pieces = lax.all_to_all(chunked, axes, 0, 0, tiled=True)
    reduced = jnp.sum(pieces, axis=0, keepdims=True)
    gathered = lax.all_to_all(jnp.broadcast_to(reduced, chunked.shape), axes, 0, 0, tiled=True)
    return gathered.reshape(value.shape)


def pair_psum(value):
    rows_n = lax.axis_size("rows")
    rel_n = lax.axis_size("rel")
    count = rows_n * rel_n
    swap = [(index, index ^ 1) for index in range(rows_n)]
    core = lax.axis_index("rows") % 2
    half = value.shape[0] // 2
    first, second = value[:half], value[half:]
    kept = jnp.where(core == 0, first, second)
    given = jnp.where(core == 0, second, first)
    chip_sum = kept + lax.ppermute(given, "rows", swap)
    pieces = lax.all_to_all(
        chip_sum.reshape((count, half // count) + value.shape[1:]), ("rows", "rel"), 0, 0, tiled=True
    )
    pieces = pieces.reshape((rows_n // 2, 2, rel_n, half // count) + value.shape[1:])
    reduced = jnp.sum(pieces, axis=(0, 2))
    outgoing = jnp.broadcast_to(reduced[None, :, None], pieces.shape).reshape(
        (count, half // count) + value.shape[1:]
    )
    own_half = lax.all_to_all(outgoing, ("rows", "rel"), 0, 0, tiled=True).reshape(
        (half,) + value.shape[1:]
    )
    other_half = lax.ppermute(own_half, "rows", swap)
    return jnp.where(
        core == 0,
        jnp.concatenate([own_half, other_half]),
        jnp.concatenate([other_half, own_half]),
    )


def permute_psum(value, axis):
    size = lax.axis_size(axis)
    me = lax.axis_index(axis)
    chunks = value.reshape((size, value.shape[0] // size) + value.shape[1:])
    total = chunks[me]
    for shift in range(1, size):
        pairs = [(index, (index + shift) % size) for index in range(size)]
        total = total + lax.ppermute(chunks[(me + shift) % size], axis, pairs)
    parts = [total]
    for shift in range(1, size):
        pairs = [(index, (index + shift) % size) for index in range(size)]
        parts.append(lax.ppermute(total, axis, pairs))
    stacked = jnp.stack(parts)
    order = (me - jnp.arange(size)) % size
    return stacked[order].reshape(value.shape)


def split_hi_lo(value):
    high = lax.optimization_barrier(value.astype(jnp.bfloat16))
    low = (value - high.astype(jnp.float32)).astype(jnp.bfloat16)
    return jnp.concatenate([high, low], axis=1)


def join_hi_lo(pair):
    half = pair.shape[1] // 2
    return pair[:, :half].astype(jnp.float32) + pair[:, half:].astype(jnp.float32)


def on_device(
    features,
    bases,
    root,
    coeffs,
    tiles,
    tile_dst,
    tile_src,
    tile_rel,
    tile_live,
    send_list,
    cotangent,
):
    highest = lax.Precision.HIGHEST
    contract_first = (((0,), (0,)), ((), ()))
    feat_width = features.shape[1]
    size_block = tiles.shape[-1]
    blocks = features.reshape(-1, size_block, feat_width)
    local_blocks = blocks.shape[0]
    num_bases = bases.shape[0]
    slots_peer = send_list.shape[-1]
    row_devices = lax.axis_size("rows")
    total_slots = row_devices * slots_peer
    count_tiles = tiles.shape[2]
    adjacency = tiles[0, 0]
    dst_ids = tile_dst[0, 0]
    src_ids = tile_src[0, 0]
    rel_ids = tile_rel[0, 0]
    live_count = tile_live[0, 0]
    send_rows = send_list[0, 0]
    step_tiles = count_tiles

    def tile_weights(first_tile):
        position = first_tile + jnp.arange(step_tiles)
        in_use = (position < live_count).astype(jnp.float32)
        rel_hot = (rel_ids[:, None] == jnp.arange(coeffs.shape[0])[None, :]).astype(jnp.float32)
        coef_rows = jnp.dot(rel_hot, coeffs, precision=highest)
        dst_hot = (dst_ids[:, None] == jnp.arange(local_blocks)[None, :]).astype(
            jnp.float32
        ) * in_use[:, None]
        return (dst_hot[:, :, None] * coef_rows[:, None, :]).reshape(
            step_tiles, local_blocks * num_bases
        )

    root_local = lax.dot_general(
        features, cotangent, contract_first, preferred_element_type=jnp.float32
    )
    root_rows = root_local.shape[0] // row_devices
    root_chunks = root_local.reshape(row_devices, root_rows, feat_width)
    outgoing = blocks[send_rows].reshape(row_devices, slots_peer * size_block, feat_width)
    outgoing = jnp.concatenate([outgoing, split_hi_lo(root_chunks)], axis=1)
    incoming = lax.all_to_all(outgoing, "rows", split_axis=0, concat_axis=0, tiled=True)
    block_rows = slots_peer * size_block
    root_mine = jnp.sum(join_hi_lo(incoming[:, block_rows:]), axis=0, keepdims=True)

    cot_blocks = cotangent.reshape(local_blocks, size_block, feat_width)
    agg_grad = jnp.einsum("lng,bfg->lbnf", cot_blocks, bases, preferred_element_type=jnp.float32)
    agg_grad = agg_grad.reshape(local_blocks * num_bases, size_block, feat_width)

    def backward_step(block_index, running):
        first_tile = block_index * step_tiles
        weights = tile_weights(first_tile)
        spread = lax.dot_general(
            weights, agg_grad, (((1,), (0,)), ((), ())), precision=highest
        ).astype(jnp.bfloat16)
        backward_term = jnp.einsum(
            "tij,tif->tjf", adjacency, spread, preferred_element_type=jnp.float32
        )
        slot_hot = (src_ids[:, None] == jnp.arange(total_slots)[None, :]).astype(jnp.float32)
        return running + lax.dot_general(
            slot_hot, backward_term, contract_first, precision=highest
        )

    slot_zero = jnp.zeros((total_slots, size_block, feat_width), jnp.float32)
    slot_grads = backward_step(0, slot_zero)
    incoming, slot_grads, root_mine = lax.optimization_barrier((incoming, slot_grads, root_mine))

    slot_out = slot_grads.astype(SLOT_GRAD_LINK_DTYPE).reshape(
        row_devices, slots_peer * size_block, feat_width
    )
    root_bcast = jnp.broadcast_to(root_mine, (row_devices,) + root_mine.shape[1:])
    slot_out = jnp.concatenate([slot_out, split_hi_lo(root_bcast)], axis=1)
    returned = lax.all_to_all(slot_out, "rows", split_axis=0, concat_axis=0, tiled=True)
    root_grad = join_hi_lo(returned[:, block_rows:]).reshape(root_local.shape)

    received = incoming[:, :block_rows].reshape(total_slots, size_block, feat_width)

    def forward_step(block_index, running):
        first_tile = block_index * step_tiles
        sources = received[src_ids]
        messages = jnp.einsum(
            "tij,tjf->tif", adjacency, sources, preferred_element_type=jnp.float32
        )
        weights = tile_weights(first_tile)
        return running + lax.dot_general(
            weights, messages, contract_first, precision=highest
        )

    zero_total = jnp.zeros((local_blocks * num_bases, size_block, feat_width), jnp.float32)
    partial_value = forward_step(0, zero_total)
    partial_value = partial_value.reshape(local_blocks, num_bases, size_block, feat_width)
    basis_f32 = bases.astype(jnp.float32)
    cot_f32 = cot_blocks.astype(jnp.float32)
    root_term = jnp.dot(features, root, preferred_element_type=jnp.float32)
    projected_part = jnp.einsum("lbnf,bfg->lng", partial_value, basis_f32, precision=highest)
    basis_local = jnp.einsum("lbnf,lng->bfg", partial_value, cot_f32, precision=highest)
    returned, basis_local, projected_part = lax.optimization_barrier(
        (returned, basis_local, projected_part)
    )

    basis_grad = pair_psum(basis_local.reshape(-1, basis_local.shape[-1])).reshape(
        basis_local.shape
    )

    block_hot = (send_rows.reshape(-1)[None, :] == jnp.arange(local_blocks)[:, None]).astype(
        jnp.float32
    )
    own_grads = lax.dot_general(
        block_hot,
        returned[:, :block_rows].astype(jnp.float32).reshape(total_slots, size_block, feat_width),
        (((1,), (0,)), ((), ())),
        precision=highest,
    )
    both = jnp.concatenate(
        [projected_part.reshape(-1, feat_width), own_grads.reshape(-1, feat_width)]
    )
    summed_both = permute_psum(both, "rel")
    projected = summed_both[: features.shape[0]]
    summed = summed_both[features.shape[0] :]
    output = (projected + root_term).astype(jnp.bfloat16)
    root_back = lax.dot_general(
        cotangent, root, (((1,), (1,)), ((), ())), preferred_element_type=jnp.float32
    )
    feature_grad = summed.reshape(-1, feat_width) + root_back
    return (output, feature_grad, basis_grad, root_grad)


def solution(mesh):
    return jax.shard_map(
        on_device,
        mesh=mesh,
        in_specs=(
            P("rows", None),
            P(),
            P(),
            P("rel", None),
            P("rows", "rel", None, None, None),
            P("rows", "rel", None),
            P("rows", "rel", None),
            P("rows", "rel", None),
            P("rows", "rel"),
            P("rows", "rel", None, None),
            P("rows", None),
        ),
        out_specs=(P("rows", None), P("rows", None), P(), P()),
        check_vma=False,
    )
```

```python
import math

import jax
import jax.numpy as jnp
from jax import lax
from jax.sharding import PartitionSpec as P

SLOT_GRAD_LINK_DTYPE = jnp.bfloat16


def a2a_psum(value, axes):
    count = 1
    for name in axes:
        count *= lax.axis_size(name)
    chunked = value.reshape((count, value.shape[0] // count) + value.shape[1:])
    pieces = lax.all_to_all(chunked, axes, 0, 0, tiled=True)
    reduced = jnp.sum(pieces, axis=0, keepdims=True)
    gathered = lax.all_to_all(jnp.broadcast_to(reduced, chunked.shape), axes, 0, 0, tiled=True)
    return gathered.reshape(value.shape)


def pair_psum(value):
    rows_n = lax.axis_size("rows")
    rel_n = lax.axis_size("rel")
    count = rows_n * rel_n
    swap = [(index, index ^ 1) for index in range(rows_n)]
    core = lax.axis_index("rows") % 2
    half = value.shape[0] // 2
    first, second = value[:half], value[half:]
    kept = jnp.where(core == 0, first, second)
    given = jnp.where(core == 0, second, first)
    chip_sum = kept + lax.ppermute(given, "rows", swap)
    pieces = lax.all_to_all(
        chip_sum.reshape((count, half // count) + value.shape[1:]), ("rows", "rel"), 0, 0, tiled=True
    )
    pieces = pieces.reshape((rows_n // 2, 2, rel_n, half // count) + value.shape[1:])
    reduced = jnp.sum(pieces, axis=(0, 2))
    outgoing = jnp.broadcast_to(reduced[None, :, None], pieces.shape).reshape(
        (count, half // count) + value.shape[1:]
    )
    own_half = lax.all_to_all(outgoing, ("rows", "rel"), 0, 0, tiled=True).reshape(
        (half,) + value.shape[1:]
    )
    other_half = lax.ppermute(own_half, "rows", swap)
    return jnp.where(
        core == 0,
        jnp.concatenate([own_half, other_half]),
        jnp.concatenate([other_half, own_half]),
    )


def permute_psum(value, axis):
    size = lax.axis_size(axis)
    me = lax.axis_index(axis)
    chunks = value.reshape((size, value.shape[0] // size) + value.shape[1:])
    total = chunks[me]
    for shift in range(1, size):
        pairs = [(index, (index + shift) % size) for index in range(size)]
        total = total + lax.ppermute(chunks[(me + shift) % size], axis, pairs)
    parts = [total]
    for shift in range(1, size):
        pairs = [(index, (index + shift) % size) for index in range(size)]
        parts.append(lax.ppermute(total, axis, pairs))
    stacked = jnp.stack(parts)
    order = (me - jnp.arange(size)) % size
    return stacked[order].reshape(value.shape)


def split_hi_lo(value):
    high = lax.optimization_barrier(value.astype(jnp.bfloat16))
    low = (value - high.astype(jnp.float32)).astype(jnp.bfloat16)
    return jnp.concatenate([high, low], axis=1)


def join_hi_lo(pair):
    half = pair.shape[1] // 2
    return pair[:, :half].astype(jnp.float32) + pair[:, half:].astype(jnp.float32)


def on_device(
    features,
    bases,
    root,
    coeffs,
    tiles,
    tile_dst,
    tile_src,
    tile_rel,
    tile_live,
    send_list,
    cotangent,
):
    highest = lax.Precision.HIGHEST
    contract_first = (((0,), (0,)), ((), ()))
    feat_width = features.shape[1]
    size_block = tiles.shape[-1]
    blocks = features.reshape(-1, size_block, feat_width)
    local_blocks = blocks.shape[0]
    num_bases = bases.shape[0]
    slots_peer = send_list.shape[-1]
    row_devices = lax.axis_size("rows")
    total_slots = row_devices * slots_peer
    count_tiles = tiles.shape[2]
    adjacency = tiles[0, 0]
    dst_ids = tile_dst[0, 0]
    src_ids = tile_src[0, 0]
    rel_ids = tile_rel[0, 0]
    live_count = tile_live[0, 0]
    send_rows = send_list[0, 0]
    step_tiles = math.gcd(count_tiles, 64)
    steps_live = (live_count + step_tiles - 1) // step_tiles

    def tile_weights(first_tile):
        position = first_tile + jnp.arange(step_tiles)
        in_use = (position < live_count).astype(jnp.float32)
        rel_hot = (rel_ids[:, None] == jnp.arange(coeffs.shape[0])[None, :]).astype(jnp.float32)
        coef_rows = jnp.dot(rel_hot, coeffs, precision=highest)
        dst_hot = (dst_ids[:, None] == jnp.arange(local_blocks)[None, :]).astype(
            jnp.float32
        ) * in_use[:, None]
        return (dst_hot[:, :, None] * coef_rows[:, None, :]).reshape(
            step_tiles, local_blocks * num_bases
        )

    root_local = lax.dot_general(
        features, cotangent, contract_first, preferred_element_type=jnp.float32
    )
    root_rows = root_local.shape[0] // row_devices
    root_chunks = root_local.reshape(row_devices, root_rows, feat_width)
    outgoing = blocks[send_rows].reshape(row_devices, slots_peer * size_block, feat_width)
    outgoing = jnp.concatenate([outgoing, split_hi_lo(root_chunks)], axis=1)
    incoming = lax.all_to_all(outgoing, "rows", split_axis=0, concat_axis=0, tiled=True)
    block_rows = slots_peer * size_block
    root_mine = jnp.sum(join_hi_lo(incoming[:, block_rows:]), axis=0, keepdims=True)

    cot_blocks = cotangent.reshape(local_blocks, size_block, feat_width)
    agg_grad = jnp.einsum("lng,bfg->lbnf", cot_blocks, bases, preferred_element_type=jnp.float32)
    agg_grad = agg_grad.reshape(local_blocks * num_bases, size_block, feat_width)

    def backward_step(block_index, running):
        first_tile = block_index * step_tiles
        weights = tile_weights(first_tile)
        spread = lax.dot_general(
            weights, agg_grad, (((1,), (0,)), ((), ())), precision=highest
        ).astype(jnp.bfloat16)
        backward_term = jnp.einsum(
            "tij,tif->tjf", adjacency, spread, preferred_element_type=jnp.float32
        )
        slot_hot = (src_ids[:, None] == jnp.arange(total_slots)[None, :]).astype(jnp.float32)
        return running + lax.dot_general(
            slot_hot, backward_term, contract_first, precision=highest
        )

    slot_zero = jnp.zeros((total_slots, size_block, feat_width), jnp.float32)
    slot_grads = lax.fori_loop(0, steps_live, backward_step, slot_zero)
    incoming, slot_grads, root_mine = lax.optimization_barrier((incoming, slot_grads, root_mine))

    slot_out = slot_grads.astype(SLOT_GRAD_LINK_DTYPE).reshape(
        row_devices, slots_peer * size_block, feat_width
    )
    root_bcast = jnp.broadcast_to(root_mine, (row_devices,) + root_mine.shape[1:])
    slot_out = jnp.concatenate([slot_out, split_hi_lo(root_bcast)], axis=1)
    returned = lax.all_to_all(slot_out, "rows", split_axis=0, concat_axis=0, tiled=True)
    root_grad = join_hi_lo(returned[:, block_rows:]).reshape(root_local.shape)

    received = incoming[:, :block_rows].reshape(total_slots, size_block, feat_width)

    def forward_step(block_index, running):
        first_tile = block_index * step_tiles
        sources = received[src_ids]
        messages = jnp.einsum(
            "tij,tjf->tif", adjacency, sources, preferred_element_type=jnp.float32
        )
        weights = tile_weights(first_tile)
        return running + lax.dot_general(
            weights, messages, contract_first, precision=highest
        )

    zero_total = jnp.zeros((local_blocks * num_bases, size_block, feat_width), jnp.float32)
    partial_value = lax.fori_loop(0, steps_live, forward_step, zero_total)
    partial_value = partial_value.reshape(local_blocks, num_bases, size_block, feat_width)
    basis_f32 = bases.astype(jnp.float32)
    cot_f32 = cot_blocks.astype(jnp.float32)
    root_term = jnp.dot(features, root, preferred_element_type=jnp.float32)
    projected_part = jnp.einsum("lbnf,bfg->lng", partial_value, basis_f32, precision=highest)
    basis_local = jnp.einsum("lbnf,lng->bfg", partial_value, cot_f32, precision=highest)
    projected = permute_psum(projected_part.reshape(-1, feat_width), "rel")
    returned, basis_local, projected = lax.optimization_barrier(
        (returned, basis_local, projected)
    )

    basis_grad = pair_psum(basis_local.reshape(-1, basis_local.shape[-1])).reshape(
        basis_local.shape
    )

    block_hot = (send_rows.reshape(-1)[None, :] == jnp.arange(local_blocks)[:, None]).astype(
        jnp.float32
    )
    own_grads = lax.dot_general(
        block_hot,
        returned[:, :block_rows].astype(jnp.float32).reshape(total_slots, size_block, feat_width),
        (((1,), (0,)), ((), ())),
        precision=highest,
    )
    summed = permute_psum(own_grads.reshape(-1, feat_width), "rel")
    output = (projected + root_term).astype(jnp.bfloat16)
    root_back = lax.dot_general(
        cotangent, root, (((1,), (1,)), ((), ())), preferred_element_type=jnp.float32
    )
    feature_grad = summed.reshape(-1, feat_width) + root_back
    return (output, feature_grad, basis_grad, root_grad)


def solution(mesh):
    return jax.shard_map(
        on_device,
        mesh=mesh,
        in_specs=(
            P("rows", None),
            P(),
            P(),
            P("rel", None),
            P("rows", "rel", None, None, None),
            P("rows", "rel", None),
            P("rows", "rel", None),
            P("rows", "rel", None),
            P("rows", "rel"),
            P("rows", "rel", None, None),
            P("rows", None),
        ),
        out_specs=(P("rows", None), P("rows", None), P(), P()),
        check_vma=False,
    )
```

```python
import math

import jax
import jax.numpy as jnp
from jax import lax
from jax.sharding import PartitionSpec as P

SLOT_GRAD_LINK_DTYPE = jnp.bfloat16


def a2a_psum(value, axes):
    count = 1
    for name in axes:
        count *= lax.axis_size(name)
    chunked = value.reshape((count, value.shape[0] // count) + value.shape[1:])
    pieces = lax.all_to_all(chunked, axes, 0, 0, tiled=True)
    reduced = jnp.sum(pieces, axis=0, keepdims=True)
    gathered = lax.all_to_all(jnp.broadcast_to(reduced, chunked.shape), axes, 0, 0, tiled=True)
    return gathered.reshape(value.shape)


def pair_first(value):
    rows_n = lax.axis_size("rows")
    swap = [(index, index ^ 1) for index in range(rows_n)]
    core = lax.axis_index("rows") % 2
    half = value.shape[0] // 2
    first, second = value[:half], value[half:]
    kept = jnp.where(core == 0, first, second)
    given = jnp.where(core == 0, second, first)
    return kept + lax.ppermute(given, "rows", swap)


def pair_psum(chip_sum, value_shape):
    value = chip_sum
    rows_n = lax.axis_size("rows")
    rel_n = lax.axis_size("rel")
    count = rows_n * rel_n
    swap = [(index, index ^ 1) for index in range(rows_n)]
    core = lax.axis_index("rows") % 2
    half = value_shape[0] // 2
    pieces = lax.all_to_all(
        chip_sum.reshape((count, half // count) + value.shape[1:]), ("rows", "rel"), 0, 0, tiled=True
    )
    pieces = pieces.reshape((rows_n // 2, 2, rel_n, half // count) + value.shape[1:])
    reduced = jnp.sum(pieces, axis=(0, 2))
    outgoing = jnp.broadcast_to(reduced[None, :, None], pieces.shape).reshape(
        (count, half // count) + value.shape[1:]
    )
    own_half = lax.all_to_all(outgoing, ("rows", "rel"), 0, 0, tiled=True).reshape(
        (half,) + value.shape[1:]
    )
    other_half = lax.ppermute(own_half, "rows", swap)
    return jnp.where(
        core == 0,
        jnp.concatenate([own_half, other_half]),
        jnp.concatenate([other_half, own_half]),
    )


def permute_psum(value, axis):
    size = lax.axis_size(axis)
    me = lax.axis_index(axis)
    chunks = value.reshape((size, value.shape[0] // size) + value.shape[1:])
    total = chunks[me]
    for shift in range(1, size):
        pairs = [(index, (index + shift) % size) for index in range(size)]
        total = total + lax.ppermute(chunks[(me + shift) % size], axis, pairs)
    parts = [total]
    for shift in range(1, size):
        pairs = [(index, (index + shift) % size) for index in range(size)]
        parts.append(lax.ppermute(total, axis, pairs))
    stacked = jnp.stack(parts)
    order = (me - jnp.arange(size)) % size
    return stacked[order].reshape(value.shape)


def split_hi_lo(value):
    high = lax.optimization_barrier(value.astype(jnp.bfloat16))
    low = (value - high.astype(jnp.float32)).astype(jnp.bfloat16)
    return jnp.concatenate([high, low], axis=1)


def join_hi_lo(pair):
    half = pair.shape[1] // 2
    return pair[:, :half].astype(jnp.float32) + pair[:, half:].astype(jnp.float32)


def on_device(
    features,
    bases,
    root,
    coeffs,
    tiles,
    tile_dst,
    tile_src,
    tile_rel,
    tile_live,
    send_list,
    cotangent,
):
    highest = lax.Precision.HIGHEST
    contract_first = (((0,), (0,)), ((), ()))
    feat_width = features.shape[1]
    size_block = tiles.shape[-1]
    blocks = features.reshape(-1, size_block, feat_width)
    local_blocks = blocks.shape[0]
    num_bases = bases.shape[0]
    slots_peer = send_list.shape[-1]
    row_devices = lax.axis_size("rows")
    total_slots = row_devices * slots_peer
    count_tiles = tiles.shape[2]
    adjacency = tiles[0, 0]
    dst_ids = tile_dst[0, 0]
    src_ids = tile_src[0, 0]
    rel_ids = tile_rel[0, 0]
    live_count = tile_live[0, 0]
    send_rows = send_list[0, 0]
    step_tiles = math.gcd(count_tiles, 64)
    steps_live = (live_count + step_tiles - 1) // step_tiles

    def tile_weights(first_tile):
        position = first_tile + jnp.arange(step_tiles)
        in_use = (position < live_count).astype(jnp.float32)
        rel_hot = (rel_ids[:, None] == jnp.arange(coeffs.shape[0])[None, :]).astype(jnp.float32)
        coef_rows = jnp.dot(rel_hot, coeffs, precision=highest)
        dst_hot = (dst_ids[:, None] == jnp.arange(local_blocks)[None, :]).astype(
            jnp.float32
        ) * in_use[:, None]
        return (dst_hot[:, :, None] * coef_rows[:, None, :]).reshape(
            step_tiles, local_blocks * num_bases
        )

    root_local = lax.dot_general(
        features, cotangent, contract_first, preferred_element_type=jnp.float32
    )
    root_rows = root_local.shape[0] // row_devices
    root_chunks = root_local.reshape(row_devices, root_rows, feat_width)
    outgoing = blocks[send_rows].reshape(row_devices, slots_peer * size_block, feat_width)
    outgoing = jnp.concatenate([outgoing, split_hi_lo(root_chunks)], axis=1)
    incoming = lax.all_to_all(outgoing, "rows", split_axis=0, concat_axis=0, tiled=True)
    block_rows = slots_peer * size_block
    root_mine = jnp.sum(join_hi_lo(incoming[:, block_rows:]), axis=0, keepdims=True)

    cot_blocks = cotangent.reshape(local_blocks, size_block, feat_width)
    agg_grad = jnp.einsum("lng,bfg->lbnf", cot_blocks, bases, preferred_element_type=jnp.float32)
    agg_grad = agg_grad.reshape(local_blocks * num_bases, size_block, feat_width)

    def backward_step(block_index, running):
        first_tile = block_index * step_tiles
        weights = tile_weights(first_tile)
        spread = lax.dot_general(
            weights, agg_grad, (((1,), (0,)), ((), ())), precision=highest
        ).astype(jnp.bfloat16)
        backward_term = jnp.einsum(
            "tij,tif->tjf", adjacency, spread, preferred_element_type=jnp.float32
        )
        slot_hot = (src_ids[:, None] == jnp.arange(total_slots)[None, :]).astype(jnp.float32)
        return running + lax.dot_general(
            slot_hot, backward_term, contract_first, precision=highest
        )

    slot_zero = jnp.zeros((total_slots, size_block, feat_width), jnp.float32)
    slot_grads = lax.fori_loop(0, steps_live, backward_step, slot_zero)
    incoming, slot_grads, root_mine = lax.optimization_barrier((incoming, slot_grads, root_mine))

    slot_out = slot_grads.astype(SLOT_GRAD_LINK_DTYPE).reshape(
        row_devices, slots_peer * size_block, feat_width
    )
    root_bcast = jnp.broadcast_to(root_mine, (row_devices,) + root_mine.shape[1:])
    slot_out = jnp.concatenate([slot_out, split_hi_lo(root_bcast)], axis=1)
    returned = lax.all_to_all(slot_out, "rows", split_axis=0, concat_axis=0, tiled=True)
    root_grad = join_hi_lo(returned[:, block_rows:]).reshape(root_local.shape)

    received = incoming[:, :block_rows].reshape(total_slots, size_block, feat_width)

    def forward_step(block_index, running):
        first_tile = block_index * step_tiles
        sources = received[src_ids]
        messages = jnp.einsum(
            "tij,tjf->tif", adjacency, sources, preferred_element_type=jnp.float32
        )
        weights = tile_weights(first_tile)
        return running + lax.dot_general(
            weights, messages, contract_first, precision=highest
        )

    zero_total = jnp.zeros((local_blocks * num_bases, size_block, feat_width), jnp.float32)
    partial_value = lax.fori_loop(0, steps_live, forward_step, zero_total)
    partial_value = partial_value.reshape(local_blocks, num_bases, size_block, feat_width)
    basis_f32 = bases.astype(jnp.float32)
    cot_f32 = cot_blocks.astype(jnp.float32)
    root_term = jnp.dot(features, root, preferred_element_type=jnp.float32)
    projected_part = jnp.einsum("lbnf,bfg->lng", partial_value, basis_f32, precision=highest)
    basis_local = jnp.einsum("lbnf,lng->bfg", partial_value, cot_f32, precision=highest)
    projected = permute_psum(projected_part.reshape(-1, feat_width), "rel")
    basis_rows = basis_local.reshape(-1, basis_local.shape[-1])
    chip_sum = pair_first(basis_rows)
    returned, chip_sum, projected = lax.optimization_barrier((returned, chip_sum, projected))

    basis_grad = pair_psum(chip_sum, basis_rows.shape).reshape(basis_local.shape)

    block_hot = (send_rows.reshape(-1)[None, :] == jnp.arange(local_blocks)[:, None]).astype(
        jnp.float32
    )
    own_grads = lax.dot_general(
        block_hot,
        returned[:, :block_rows].astype(jnp.float32).reshape(total_slots, size_block, feat_width),
        (((1,), (0,)), ((), ())),
        precision=highest,
    )
    summed = permute_psum(own_grads.reshape(-1, feat_width), "rel")
    output = (projected + root_term).astype(jnp.bfloat16)
    root_back = lax.dot_general(
        cotangent, root, (((1,), (1,)), ((), ())), preferred_element_type=jnp.float32
    )
    feature_grad = summed.reshape(-1, feat_width) + root_back
    return (output, feature_grad, basis_grad, root_grad)


def solution(mesh):
    return jax.shard_map(
        on_device,
        mesh=mesh,
        in_specs=(
            P("rows", None),
            P(),
            P(),
            P("rel", None),
            P("rows", "rel", None, None, None),
            P("rows", "rel", None),
            P("rows", "rel", None),
            P("rows", "rel", None),
            P("rows", "rel"),
            P("rows", "rel", None, None),
            P("rows", None),
        ),
        out_specs=(P("rows", None), P("rows", None), P(), P()),
        check_vma=False,
    )
```
